128 devices in a mesh: row: 8 (over y, core), col: 16 (over z, x).
Axes of the slice: x: 4, y: 4, z: 4, core: 2. Of those that a mesh axis runs over, the one named last changes fastest.
Arguments:
- noisy: float32 [2048, 16384], P('row', 'col'), may hold values from -7 to 7
- fidelity: float32 [2048, 16384], P('row', 'col'), may hold values from 2 to 20
Outputs:
- denoised: float32 [2048, 16384], P('row', 'col')
- dual: float32 [2, 2048, 16384], P(None, 'row', 'col')
- final_tau: float32 [], replicated
The draws below stay inside these ranges and needn't reach their ends.
All inputs are finite; a program needn't handle non-finite values.
Results may differ from the reference program's by a relative error of at most 0.0001.
Values sent between devices are 32-bit elements; how exact they have to be, the bound alone decides.
A program may use at most 64 MiB of HBM per device.

```python
import math
import jax
import jax.numpy as jnp

ITERS = 4
NR = 2048
NC = 16384


def draw_noisy(key, part):
    rows = (jnp.arange(NR, dtype=jnp.float32) / NR)[:, None]
    cols = (jnp.arange(NC, dtype=jnp.float32) / NC)[None, :]
    spread = 0.15 * (1.0 + 2.0 * rows) * (1.0 + 2.0 * cols)
    clean = 0.8 * jnp.sin(6.2831853 * 3.0 * rows + 1.0) * jnp.cos(6.2831853 * 5.0 * cols)
    noise = jnp.clip(jax.random.normal(key, (NR, NC), jnp.float32), -4.0, 4.0)
    return (clean + spread * noise).astype(jnp.float32)


def steps_of(key, extent, cuts, least, largest):
    def one(dim, blocks):
        steps = jax.random.uniform(jax.random.fold_in(jax.random.fold_in(key, 6), dim), (blocks,), jnp.float32, least / len(cuts), largest / len(cuts))
        return jnp.repeat(jnp.exp(steps), extent[dim] // blocks).reshape((-1,) + (1,) * (len(extent) - dim - 1))

    loudness = one(*cuts[0])
    for cut in cuts[1:]:
        loudness = loudness * one(*cut)
    return loudness


def setup_inputs(seed: int = 0) -> dict:
    seeds = jax.random.split(jax.random.key(seed), 3)
    noisy = draw_noisy(jax.random.fold_in(seeds[2], 71), 0)
    fidelity = jnp.clip(jnp.exp(math.log(20.0) - 2.3025851 * jax.random.uniform(seeds[1], (NR, NC), jnp.float32) ** steps_of(seeds[1], (NR, NC), ((0, 8), (1, 16)), -0.2, 0.2)), 2.0, 20.0)
    return {"noisy": noisy, "fidelity": fidelity}


first_tau = 0.35
step_product = 0.124
adapt_rate = 0.5
adapt_decay = 0.9
epsilon = 1e-06

def forward(field):
    zero_row = jnp.zeros((1, field.shape[1]), jnp.float32)
    zero_col = jnp.zeros((field.shape[0], 1), jnp.float32)
    grad_x = jnp.concatenate([field[1:] - field[:-1], zero_row], axis=0)
    grad_y = jnp.concatenate([field[:, 1:] - field[:, :-1], zero_col], axis=1)
    return (grad_x, grad_y)

def backward(dual_x, dual_y):
    zero_row = jnp.zeros((1, dual_x.shape[1]), jnp.float32)
    zero_col = jnp.zeros((dual_y.shape[0], 1), jnp.float32)
    part_x = dual_x - jnp.concatenate([zero_row, dual_x[:-1]], axis=0)
    part_y = dual_y - jnp.concatenate([zero_col, dual_y[:, :-1]], axis=1)
    return part_x + part_y

def reference(noisy, fidelity):
    cells = jnp.float32(NR * NC)
    current = noisy
    extrapolated = noisy
    dual_x = jnp.zeros_like(noisy)
    dual_y = jnp.zeros_like(noisy)
    div_prev = jnp.zeros_like(noisy)
    tau = jnp.float32(first_tau)
    sigma = jnp.float32(step_product) / tau
    for step in range(ITERS):
        grad_x, grad_y = forward(extrapolated)
        moved_x = dual_x + sigma * grad_x
        moved_y = dual_y + sigma * grad_y
        shrink = jnp.maximum(1.0, jnp.sqrt(moved_x * moved_x + moved_y * moved_y))
        new_x = moved_x / shrink
        new_y = moved_y / shrink
        div_new = backward(new_x, new_y)
        updated = (current + tau * div_new + tau * fidelity * noisy) / (1.0 + tau * fidelity)
        change = current - updated
        change_x, change_y = forward(change)
        primal = jnp.sum(jnp.abs(change / tau + div_prev - div_new))
        dualres = jnp.sum(jnp.abs((dual_x - new_x) / sigma - change_x)) + jnp.sum(jnp.abs((dual_y - new_y) / sigma - change_y))
        ratio = jnp.log((primal / cells + epsilon) / (dualres / cells + epsilon))
        tau = tau * jnp.exp(adapt_rate * adapt_decay ** step * ratio / (1.0 + jnp.abs(ratio)))
        sigma = jnp.float32(step_product) / tau
        extrapolated = 2.0 * updated - current
        current = updated
        dual_x, dual_y = (new_x, new_y)
        div_prev = div_new
    return (current, jnp.stack([dual_x, dual_y]), tau)
```

```python
import functools
import jax
import jax.numpy as jnp
import numpy as np
from jax import lax
from jax.experimental import pallas as pl
from jax.experimental.pallas import tpu as pltpu
from jax.sharding import PartitionSpec as P

ITERS = 4
MESH = pl.DeviceIdType.MESH

first_tau = np.float32(0.35)
step_product = np.float32(0.124)
adapt_rate = 0.5
adapt_decay = 0.9
epsilon = np.float32(1e-06)

SUB = 8
LANE = 128
UNROLL = 3


def kernel(
    n_row, n_col, cells,
    noisy_hbm, fid_hbm,
    u_out, dual_out, tau_out,
    U, F, FN, UB, PX, PY, GX, GY, DV, QT, CB, rb1, rb2,
    load_sem, halo_send, halo_recv, red_send, red_recv,
):
    rows, cols = noisy_hbm.shape
    strips = rows // SUB + 2
    tiles = cols // LANE
    my_row, my_col = lax.axis_index("row"), lax.axis_index("col")
    f32 = jnp.float32

    def row_at(d):
        return lax.rem(my_row + d + n_row, n_row)

    def col_at(d):
        return lax.rem(my_col + d + n_col, n_col)

    sub = lax.broadcasted_iota(jnp.int32, (SUB, LANE), 0)
    lane = lax.broadcasted_iota(jnp.int32, (SUB, LANE), 1)
    sub_first, sub_last = sub == 0, sub == SUB - 1
    lane_first, lane_last = lane == 0, lane == LANE - 1

    CB[...] = jnp.zeros_like(CB)

    loads = [
        pltpu.make_async_copy(src, dst.at[SUB : SUB + rows, 0:cols], load_sem.at[i])
        for i, (src, dst) in enumerate(((noisy_hbm, U), (fid_hbm, F)))
    ]
    for load in loads:
        load.start()
    barrier = pltpu.get_barrier_semaphore()
    partners = [(row_at(d), my_col) for d in range(1, n_row)]
    partners += [(my_row, col_at(d)) for d in range(1, n_col)]
    partners += [(row_at(a), col_at(b)) for a in (-1, 1) for b in (-1, 1)]
    for partner in partners:
        pl.semaphore_signal(barrier, inc=1, device_id=partner, device_id_type=MESH)
    for load in loads:
        load.wait()

    def pack(b):
        at = pl.ds(SUB + b * LANE, LANE)
        lanes = lax.broadcasted_iota(jnp.int32, (LANE, LANE), 1)
        n0, n7 = U[at, 0:LANE], U[at, cols - LANE : cols]
        f0 = pltpu.roll(F[at, 0:LANE], 8, axis=1)
        f7 = pltpu.roll(F[at, cols - LANE : cols], LANE - 8, axis=1)
        low = jnp.where(lanes < 8, n0, f0)
        high = jnp.where(lanes >= LANE - 8, n7, f7)
        return jnp.where(lanes < LANE // 2, low, high).T

    for b in range(rows // LANE):
        QT[:, b * LANE : (b + 1) * LANE] = pack(b)

    pl.semaphore_wait(barrier, len(partners))

    low, high = slice(0, 16), slice(LANE - 16, LANE)
    mid = slice(LANE, LANE + rows)
    top, bottom = slice(0, LANE), slice(LANE + rows, 2 * LANE + rows)
    first, last = slice(0, LANE), slice(rows - LANE, rows)
    below_rows = slice(rows + SUB, rows + 2 * SUB)
    moves = []
    for src, dst in ((noisy_hbm, U), (fid_hbm, F)):
        moves.append((src.at[0:SUB, :], dst.at[below_rows, 0:cols], -1, 0))
        moves.append((src.at[rows - SUB : rows, :], dst.at[0:SUB, 0:cols], 1, 0))
    moves.append((QT.at[low, :], CB.at[low, mid], 0, -1))
    moves.append((QT.at[high, :], CB.at[high, mid], 0, 1))
    for side, step in ((low, -1), (high, 1)):
        moves.append((QT.at[side, last], CB.at[side, top], 1, step))
        moves.append((QT.at[side, first], CB.at[side, bottom], -1, step))
    halos = [
        pltpu.make_async_remote_copy(
            src_ref=src, dst_ref=dst, send_sem=halo_send.at[i], recv_sem=halo_recv.at[i],
            device_id=(row_at(a), col_at(b)), device_id_type=MESH,
        )
        for i, (src, dst, a, b) in enumerate(moves)
    ]
    for halo in halos:
        halo.start()
    for halo in halos:
        halo.wait_recv()

    def unpack(block, start, count, to):
        turned = block.T[start : start + count, :]
        lanes = lax.broadcasted_iota(jnp.int32, turned.shape, 1)
        edge = jnp.logical_or(lanes < 8, lanes >= LANE - 8)
        fid = jnp.where(
            lanes < LANE // 2, pltpu.roll(turned, LANE - 8, axis=1), pltpu.roll(turned, 8, axis=1)
        )
        U[to : to + count, cols : cols + LANE] = jnp.where(edge, turned, 0.0)
        F[to : to + count, cols : cols + LANE] = jnp.where(edge, fid, 1.0)

    unpack(CB[:, top], LANE - SUB, SUB, 0)
    for b in range(rows // LANE):
        unpack(CB[:, (b + 1) * LANE : (b + 2) * LANE], 0, LANE, SUB + b * LANE)
    unpack(CB[:, bottom], 0, SUB, SUB + rows)

    def at(s, c):
        start = s * SUB if isinstance(s, int) else pl.multiple_of(s * SUB, SUB)
        return pl.ds(start, SUB), slice(c * LANE, (c + 1) * LANE)

    at_left, at_right = my_col == 0, my_col == n_col - 1
    last_col = jnp.logical_and(at_right, lane_last)
    outside = jnp.logical_and(at_left, lane >= LANE // 2)
    in_first_row = jnp.logical_and(my_row == 0, sub_first)

    def gradient(field, extra):
        def body(s, carry):
            cell = my_row * rows + (s - 1) * SUB + sub
            inside = jnp.logical_and(cell >= 0, cell < n_row * rows - 1)
            after = jnp.minimum(s + 1, strips - 1)
            here = [field[at(s, c)] for c in range(tiles + 1)]
            turned = [pltpu.roll(h, LANE - 1, axis=1) for h in here]
            for c in range(tiles + 1):
                below = jnp.where(
                    sub_last,
                    pltpu.roll(field[at(after, c)], SUB - 1, axis=0),
                    pltpu.roll(here[c], SUB - 1, axis=0),
                )
                right = jnp.where(lane_last, turned[(c + 1) % (tiles + 1)], turned[c])
                gx = jnp.where(inside, below - here[c], 0.0)
                gy = right - here[c]
                if c == tiles - 1:
                    gy = jnp.where(last_col, 0.0, gy)
                if c == tiles:
                    gy = jnp.where(outside, 0.0, gy)
                GX[at(s, c)] = gx
                GY[at(s, c)] = gy
                if extra:
                    FN[at(s, c)] = F[at(s, c)] * here[c]
            return carry

        lax.fori_loop(0, strips, body, 0)

    gradient(U, True)

    def strip(k, s, carry, counted, tau, sigma, itau, isigma):
        prev_x, prev_w, acc_p, acc_d, acc_l = carry
        prev_x, prev_w = list(prev_x), list(prev_w)
        final = k == ITERS - 1
        first_strip = isinstance(s, int) and s == 1

        def dual_step(c):
            qx, qy = sigma * GX[at(s, c)], sigma * GY[at(s, c)]
            if k:
                px, py = PX[at(s, c)], PY[at(s, c)]
                qx, qy = px + qx, py + qy
            scale = lax.rsqrt(jnp.maximum(qx * qx + qy * qy, 1.0))
            nx, ny = qx * scale, qy * scale
            tx, ty = ((px - nx) * isigma, (py - ny) * isigma) if k else (-nx * isigma, -ny * isigma)
            return nx, ny, tx, ty, pltpu.roll(nx, 1, axis=0), pltpu.roll(ny, 1, axis=1)

        def primal_step(c, dual, left):
            nx, ny, tx, ty, rx, ry = dual
            div = (nx - jnp.where(sub_first, prev_x[c], rx)) + (ny - jnp.where(lane_first, left, ry))
            prev_x[c] = rx
            old = U[at(s, c)]
            new = (old + tau * (div + FN[at(s, c)])) / (1.0 + tau * F[at(s, c)])
            du = old - new
            wx, wy = tx + du, ty + du
            before = DV[at(s, c)] if k and counted and c < tiles else None
            if not final:
                PX[at(s, c)] = nx
                PY[at(s, c)] = ny
                U[at(s, c)] = new
                UB[at(s, c)] = 2.0 * new - old
                DV[at(s, c)] = div
            elif counted and c < tiles:
                own = at(s - 1, c)
                u_out[own] = new
                dual_out[(0, *own)] = nx
                dual_out[(1, *own)] = ny
            rwx, rwy = pltpu.roll(wx, 1, axis=0), pltpu.roll(wy, 1, axis=1)
            upper = prev_w[c]
            prev_w[c] = rwx
            return div, du, before, upper, rwx, rwy

        def residual(got, left):
            div, du, before, upper, rwx, rwy = got
            primal = du * itau - div
            if before is not None:
                primal = primal + before
            return (
                jnp.abs(primal),
                jnp.abs(jnp.where(sub_first, upper, rwx) - du),
                jnp.abs(jnp.where(lane_first, left, rwy) - du),
            )

        before_last = dual_step(tiles - 1)
        halo = dual_step(tiles)
        halo_got = primal_step(tiles, halo, before_last[5])
        left, left_w = halo[5], halo_got[5]
        for c in range(tiles):
            dual = before_last if c == tiles - 1 else dual_step(c)
            got = primal_step(c, dual, left)
            if counted:
                primal, along, across = residual(got, left_w)
                if first_strip:
                    along = jnp.where(in_first_row, 0.0, along)
                acc_p = acc_p + primal
                if c == 0:
                    acc_l = acc_l + across
                    acc_d = acc_d + along
                else:
                    acc_d = acc_d + (along + across)
            left, left_w = dual[5], got[5]
        return tuple(prev_x), tuple(prev_w), acc_p, acc_d, acc_l

    def reduce_start(k, primal, dual):
        rb1[k, my_row, 0:1, :] = jnp.sum(primal, axis=0, keepdims=True)
        rb1[k, my_row, 1:2, :] = jnp.sum(dual, axis=0, keepdims=True)
        for d in range(1, n_row):
            pltpu.make_async_remote_copy(
                src_ref=rb1.at[k, my_row], dst_ref=rb1.at[k, my_row],
                send_sem=red_send.at[k, 0], recv_sem=red_recv.at[k, 0],
                device_id=(row_at(d), my_col), device_id_type=MESH,
            ).start()

    def reduce_middle(k):
        got = rb1.at[k, 0 : n_row - 1]
        pltpu.make_async_copy(got, got, red_recv.at[k, 0]).wait()
        total = rb1[k, 0]
        for i in range(1, n_row):
            total = total + rb1[k, i]
        rb2[k, my_col] = total
        for d in range(1, n_col):
            pltpu.make_async_remote_copy(
                src_ref=rb2.at[k, my_col], dst_ref=rb2.at[k, my_col],
                send_sem=red_send.at[k, 1], recv_sem=red_recv.at[k, 1],
                device_id=(my_row, col_at(d)), device_id_type=MESH,
            ).start()

    def reduce_end(k):
        got = rb2.at[k, 0 : n_col - 1]
        pltpu.make_async_copy(got, got, red_recv.at[k, 1]).wait()
        total = rb2[k, 0]
        for i in range(1, n_col):
            total = total + rb2[k, i]
        total = jnp.sum(total, axis=1, keepdims=True)
        return total[0:1], total[1:2]

    zero = jnp.zeros((SUB, LANE), f32)
    tau_one = jnp.full((1, 1), first_tau, f32)
    sigma_one = jnp.full((1, 1), step_product / first_tau, f32)
    for k in range(ITERS):
        def full(x):
            return jnp.broadcast_to(x, (SUB, LANE))

        steps = (full(tau_one), full(sigma_one), full(1.0 / tau_one), full(1.0 / sigma_one))
        none = (zero,) * (tiles + 1)
        carry = strip(k, 0, (none, none, zero, zero, zero), False, *steps)
        carry = strip(k, 1, carry, True, *steps)

        def body(i, carry, k=k, steps=steps):
            for j in range(UNROLL):
                carry = strip(k, 2 + i * UNROLL + j, carry, True, *steps)
            return carry

        whole = (strips - 3) // UNROLL
        carry = lax.fori_loop(0, whole, body, carry)
        for s in range(2 + whole * UNROLL, strips - 1):
            carry = strip(k, s, carry, True, *steps)
        if k < ITERS - 1:
            carry = strip(k, strips - 1, carry, False, *steps)
        _, _, primal, dual, at_first = carry
        dual = dual + jnp.where(jnp.logical_and(at_left, lane_first), 0.0, at_first)
        reduce_start(k, primal, dual)
        reduce_middle(k)
        if k < ITERS - 1:
            gradient(UB, False)
        primal, dual = reduce_end(k)
        ratio = jnp.log((primal / cells + epsilon) / (dual / cells + epsilon))
        rate = np.float32(adapt_rate * adapt_decay**k)
        tau_one = tau_one * jnp.exp(rate * ratio / (1.0 + jnp.abs(ratio)))
        sigma_one = step_product / tau_one
    tau_out[...] = jnp.broadcast_to(tau_one, tau_out.shape)

    for halo in halos:
        halo.wait_send()
    for k in range(ITERS):
        sent = rb1.at[k, 0 : n_row - 1]
        pltpu.make_async_copy(sent, sent, red_send.at[k, 0]).wait()
        sent = rb2.at[k, 0 : n_col - 1]
        pltpu.make_async_copy(sent, sent, red_send.at[k, 1]).wait()


def solution(mesh):
    n_row, n_col = mesh.shape["row"], mesh.shape["col"]

    def on_device(noisy, fidelity):
        rows, cols = noisy.shape
        f32 = jnp.float32
        padded = pltpu.VMEM((rows + 2 * SUB, cols + LANE), f32)
        cells = np.float32(rows * cols * n_row * n_col)
        vmem = pl.BlockSpec(memory_space=pltpu.VMEM)
        current, dual, tau = pl.pallas_call(
            functools.partial(kernel, n_row, n_col, cells),
            out_shape=(
                jax.ShapeDtypeStruct((rows, cols), f32),
                jax.ShapeDtypeStruct((2, rows, cols), f32),
                jax.ShapeDtypeStruct((1, LANE), f32),
            ),
            in_specs=[pl.BlockSpec(memory_space=pl.ANY)] * 2,
            out_specs=(vmem, vmem, vmem),
            scratch_shapes=[padded] * 9
            + [
                pltpu.VMEM((LANE, rows), f32),
                pltpu.VMEM((LANE, rows + 2 * LANE), f32),
                pltpu.VMEM((ITERS, n_row, 2, LANE), f32),
                pltpu.VMEM((ITERS, n_col, 2, LANE), f32),
                pltpu.SemaphoreType.DMA((2,)),
                pltpu.SemaphoreType.DMA((10,)),
                pltpu.SemaphoreType.DMA((10,)),
                pltpu.SemaphoreType.DMA((ITERS, 2)),
                pltpu.SemaphoreType.DMA((ITERS, 2)),
            ],
            compiler_params=pltpu.CompilerParams(
                collective_id=0, has_side_effects=True, vmem_limit_bytes=40 * 1024 * 1024
            ),
        )(noisy, fidelity)
        return current, dual, tau[0, 0]

    return jax.shard_map(
        on_device,
        mesh=mesh,
        in_specs=(P("row", "col"), P("row", "col")),
        out_specs=(P("row", "col"), P(None, "row", "col"), P()),
        check_vma=False,
    )
```

```python
import functools
import jax
import jax.numpy as jnp
import numpy as np
from jax import lax
from jax.experimental import pallas as pl
from jax.experimental.pallas import tpu as pltpu
from jax.sharding import PartitionSpec as P

ITERS = 4
MESH = pl.DeviceIdType.MESH

first_tau = np.float32(0.35)
step_product = np.float32(0.124)
adapt_rate = 0.5
adapt_decay = 0.9
epsilon = np.float32(1e-06)

SUB = 8
LANE = 128
UNROLL = 3


def kernel(
    n_row, n_col, cells,
    noisy_hbm, fid_hbm,
    u_out, dual_out, tau_out,
    N, F, U, H, UB, PX, PY, GX, GY, DV, QT, CB, rb,
    load_sem, halo_send, halo_recv, red_send, red_recv,
):
    rows, cols = noisy_hbm.shape
    strips = rows // SUB + 2
    tiles = cols // LANE
    my_row, my_col = lax.axis_index("row"), lax.axis_index("col")
    f32 = jnp.float32

    def distance(ab):
        a, b = ab
        return sum(min(v % 4, 4 - v % 4) for v in (a // 2, b // 4, b % 4))

    def row_at(d):
        return lax.rem(my_row + d + n_row, n_row)

    def col_at(d):
        return lax.rem(my_col + d + n_col, n_col)

    sub = lax.broadcasted_iota(jnp.int32, (SUB, LANE), 0)
    lane = lax.broadcasted_iota(jnp.int32, (SUB, LANE), 1)
    sub_first, sub_last = sub == 0, sub == SUB - 1
    lane_first, lane_last = lane == 0, lane == LANE - 1

    def at(s, c):
        start = s * SUB if isinstance(s, int) else pl.multiple_of(s * SUB, SUB)
        return pl.ds(start, SUB), slice(c * LANE, (c + 1) * LANE)

    at_left, at_right = my_col == 0, my_col == n_col - 1
    last_col = jnp.logical_and(at_right, lane_last)
    outside = jnp.logical_and(at_left, lane >= LANE // 2)
    in_first_row = jnp.logical_and(my_row == 0, sub_first)

    def gradient_strip(field, s, which):
        cell = my_row * rows + (s - 1) * SUB + sub
        inside = jnp.logical_and(cell >= 0, cell < n_row * rows - 1)
        after = min(s + 1, strips - 1) if isinstance(s, int) else jnp.minimum(s + 1, strips - 1)
        here = {c: field[at(s, c)] for c in {c for w in which for c in (w, (w + 1) % (tiles + 1))}}
        turned = {c: pltpu.roll(h, LANE - 1, axis=1) for c, h in here.items()}
        for c in which:
            below = jnp.where(
                sub_last,
                pltpu.roll(field[at(after, c)], SUB - 1, axis=0),
                pltpu.roll(here[c], SUB - 1, axis=0),
            )
            right = jnp.where(lane_last, turned[(c + 1) % (tiles + 1)], turned[c])
            gx = jnp.where(inside, below - here[c], 0.0)
            gy = right - here[c]
            if c == tiles - 1:
                gy = jnp.where(last_col, 0.0, gy)
            if c == tiles:
                gy = jnp.where(outside, 0.0, gy)
            GX[at(s, c)] = gx
            GY[at(s, c)] = gy

    everywhere = tuple(range(tiles + 1))

    def between(s, carry):
        gradient_strip(UB, s, everywhere)
        for c in everywhere:
            H[at(s, c)] = F[at(s, c)] * (U[at(s, c)] - N[at(s, c)])
        return carry

    CB[...] = jnp.zeros_like(CB)

    loads = [
        pltpu.make_async_copy(src, dst.at[SUB : SUB + rows, 0:cols], load_sem.at[i])
        for i, (src, dst) in enumerate(((noisy_hbm, N), (fid_hbm, F)))
    ]
    for load in loads:
        load.start()
    barrier = pltpu.get_barrier_semaphore()
    offsets = [(a, b) for a in range(n_row) for b in range(n_col) if a or b]
    offsets.sort(key=lambda ab: -distance(ab))
    partners = [(row_at(a), col_at(b)) for a, b in offsets]
    for partner in partners:
        pl.semaphore_signal(barrier, inc=1, device_id=partner, device_id_type=MESH)
    for load in loads:
        load.wait()

    def pack(b):
        at = pl.ds(SUB + b * LANE, LANE)
        lanes = lax.broadcasted_iota(jnp.int32, (LANE, LANE), 1)
        n0, n7 = N[at, 0:LANE], N[at, cols - LANE : cols]
        f0 = pltpu.roll(F[at, 0:LANE], 8, axis=1)
        f7 = pltpu.roll(F[at, cols - LANE : cols], LANE - 8, axis=1)
        low = jnp.where(lanes < 8, n0, f0)
        high = jnp.where(lanes >= LANE - 8, n7, f7)
        return jnp.where(lanes < LANE // 2, low, high).T

    for b in range(rows // LANE):
        QT[:, b * LANE : (b + 1) * LANE] = pack(b)

    pl.semaphore_wait(barrier, len(partners))

    low, high = slice(0, 16), slice(LANE - 16, LANE)
    mid = slice(LANE, LANE + rows)
    top, bottom = slice(0, LANE), slice(LANE + rows, 2 * LANE + rows)
    first, last = slice(0, LANE), slice(rows - LANE, rows)
    below_rows = slice(rows + SUB, rows + 2 * SUB)
    moves = []
    for src, dst in ((noisy_hbm, N), (fid_hbm, F)):
        moves.append((src.at[0:SUB, :], dst.at[below_rows, 0:cols], -1, 0))
        moves.append((src.at[rows - SUB : rows, :], dst.at[0:SUB, 0:cols], 1, 0))
    moves.append((QT.at[low, :], CB.at[low, mid], 0, -1))
    moves.append((QT.at[high, :], CB.at[high, mid], 0, 1))
    for side, step in ((low, -1), (high, 1)):
        moves.append((QT.at[side, last], CB.at[side, top], 1, step))
        moves.append((QT.at[side, first], CB.at[side, bottom], -1, step))
    halos = [
        pltpu.make_async_remote_copy(
            src_ref=src, dst_ref=dst, send_sem=halo_send.at[i], recv_sem=halo_recv.at[i],
            device_id=(row_at(a), col_at(b)), device_id_type=MESH,
        )
        for i, (src, dst, a, b) in enumerate(moves)
    ]
    for halo in halos:
        halo.start()

    def interior(s, carry):
        gradient_strip(N, s, everywhere[: tiles - 1])
        return carry

    lax.fori_loop(1, strips - 2, interior, 0)

    for halo in halos:
        halo.wait_recv()

    def unpack(block, start, count, to):
        turned = block.T[start : start + count, :]
        lanes = lax.broadcasted_iota(jnp.int32, turned.shape, 1)
        edge = jnp.logical_or(lanes < 8, lanes >= LANE - 8)
        fid = jnp.where(
            lanes < LANE // 2, pltpu.roll(turned, LANE - 8, axis=1), pltpu.roll(turned, 8, axis=1)
        )
        N[to : to + count, cols : cols + LANE] = jnp.where(edge, turned, 0.0)
        F[to : to + count, cols : cols + LANE] = jnp.where(edge, fid, 1.0)

    unpack(CB[:, top], LANE - SUB, SUB, 0)
    for b in range(rows // LANE):
        unpack(CB[:, (b + 1) * LANE : (b + 2) * LANE], 0, LANE, SUB + b * LANE)
    unpack(CB[:, bottom], 0, SUB, SUB + rows)

    def border(s, carry):
        gradient_strip(N, s, everywhere[tiles - 1 :])
        return carry

    lax.fori_loop(1, strips - 2, border, 0)
    for s in (0, strips - 2, strips - 1):
        gradient_strip(N, s, everywhere)

    def strip(k, s, carry, counted, tau, sigma, itau, isigma):
        prev_x, prev_w, acc_p, acc_d, acc_l = carry
        prev_x, prev_w = list(prev_x), list(prev_w)
        final = k == ITERS - 1
        first_strip = isinstance(s, int) and s == 1

        def dual_step(c):
            qx, qy = sigma * GX[at(s, c)], sigma * GY[at(s, c)]
            if k:
                px, py = PX[at(s, c)], PY[at(s, c)]
                qx, qy = px + qx, py + qy
            scale = lax.rsqrt(jnp.maximum(qx * qx + qy * qy, 1.0))
            nx, ny = qx * scale, qy * scale
            tx, ty = (px - nx, py - ny) if k else (-nx, -ny)
            return nx, ny, tx, ty, pltpu.roll(nx, 1, axis=0), pltpu.roll(ny, 1, axis=1)

        def primal_step(c, dual, left):
            nx, ny, tx, ty, rx, ry = dual
            div = (nx - jnp.where(sub_first, prev_x[c], rx)) + (ny - jnp.where(lane_first, left, ry))
            prev_x[c] = rx
            if k:
                old = U[at(s, c)]
                du = (H[at(s, c)] - div) / (itau + F[at(s, c)])
            else:
                old = N[at(s, c)]
                du = div / (-itau - F[at(s, c)])
            new = old - du
            scaled = sigma * du
            wx, wy = tx + scaled, ty + scaled
            before = DV[at(s, c)] if k and counted and c < tiles else None
            if not final:
                PX[at(s, c)] = nx
                PY[at(s, c)] = ny
                U[at(s, c)] = new
                UB[at(s, c)] = new - du
                if c < tiles:
                    DV[at(s, c)] = div
            elif counted and c < tiles:
                own = at(s - 1, c)
                u_out[own] = new
                dual_out[(0, *own)] = nx
                dual_out[(1, *own)] = ny
            rwx, rwy = pltpu.roll(wx, 1, axis=0), pltpu.roll(wy, 1, axis=1)
            upper = prev_w[c]
            prev_w[c] = rwx
            return div, du, scaled, before, upper, rwx, rwy

        def residual(got, left):
            div, du, scaled, before, upper, rwx, rwy = got
            primal = du * itau - div
            if before is not None:
                primal = primal + before
            return (
                jnp.abs(primal),
                jnp.abs(jnp.where(sub_first, upper, rwx) - scaled),
                jnp.abs(jnp.where(lane_first, left, rwy) - scaled),
            )

        before_last = dual_step(tiles - 1)
        halo = dual_step(tiles)
        halo_got = primal_step(tiles, halo, before_last[5])
        left, left_w = halo[5], halo_got[6]
        for c in range(tiles):
            dual = before_last if c == tiles - 1 else dual_step(c)
            got = primal_step(c, dual, left)
            if counted:
                primal, along, across = residual(got, left_w)
                if first_strip:
                    along = jnp.where(in_first_row, 0.0, along)
                acc_p = acc_p + primal
                if c == 0:
                    acc_l = acc_l + across
                    acc_d = acc_d + along
                else:
                    acc_d = acc_d + (along + across)
            left, left_w = dual[5], got[6]
        return tuple(prev_x), tuple(prev_w), acc_p, acc_d, acc_l

    me = my_row * n_col + my_col
    others = len(offsets)

    def reduce_start(k, primal, dual):
        rb[k, me, 0:1, :] = jnp.sum(primal, axis=0, keepdims=True)
        rb[k, me, 1:2, :] = jnp.sum(dual, axis=0, keepdims=True)
        for partner in partners:
            pltpu.make_async_remote_copy(
                src_ref=rb.at[k, me], dst_ref=rb.at[k, me],
                send_sem=red_send.at[k], recv_sem=red_recv.at[k],
                device_id=partner, device_id_type=MESH,
            ).start()

    def reduce_end(k):
        got = rb.at[k, 0:others]
        pltpu.make_async_copy(got, got, red_recv.at[k]).wait()
        parts = [rb[k, i] for i in range(others + 1)]
        while len(parts) > 1:
            parts = [a + b for a, b in zip(parts[::2], parts[1::2])]
        total = jnp.sum(parts[0], axis=1, keepdims=True)
        return total[0:1], total[1:2]

    zero = jnp.zeros((SUB, LANE), f32)
    tau_one = jnp.full((1, 1), first_tau, f32)
    sigma_one = jnp.full((1, 1), step_product / first_tau, f32)
    for k in range(ITERS):
        def full(x):
            return jnp.broadcast_to(x, (SUB, LANE))

        steps = (full(tau_one), full(sigma_one), full(1.0 / tau_one), full(1.0 / sigma_one))
        none = (zero,) * (tiles + 1)
        carry = strip(k, 0, (none, none, zero, zero, zero), False, *steps)
        carry = strip(k, 1, carry, True, *steps)

        def body(i, carry, k=k, steps=steps):
            for j in range(UNROLL):
                carry = strip(k, 2 + i * UNROLL + j, carry, True, *steps)
            return carry

        whole = (strips - 3) // UNROLL
        carry = lax.fori_loop(0, whole, body, carry)
        for s in range(2 + whole * UNROLL, strips - 1):
            carry = strip(k, s, carry, True, *steps)
        if k < ITERS - 1:
            carry = strip(k, strips - 1, carry, False, *steps)
        _, _, primal, dual, at_first = carry
        dual = dual + jnp.where(jnp.logical_and(at_left, lane_first), 0.0, at_first)
        reduce_start(k, primal, dual * steps[3])
        if k < ITERS - 1:
            lax.fori_loop(0, strips, between, 0)
        primal, dual = reduce_end(k)
        ratio = jnp.log((primal / cells + epsilon) / (dual / cells + epsilon))
        rate = np.float32(adapt_rate * adapt_decay**k)
        tau_one = tau_one * jnp.exp(rate * ratio / (1.0 + jnp.abs(ratio)))
        sigma_one = step_product / tau_one
    tau_out[...] = jnp.broadcast_to(tau_one, tau_out.shape)

    for halo in halos:
        halo.wait_send()
    for k in range(ITERS):
        sent = rb.at[k, 0:others]
        pltpu.make_async_copy(sent, sent, red_send.at[k]).wait()


def solution(mesh):
    n_row, n_col = mesh.shape["row"], mesh.shape["col"]

    def on_device(noisy, fidelity):
        rows, cols = noisy.shape
        f32 = jnp.float32
        padded = pltpu.VMEM((rows + 2 * SUB, cols + LANE), f32)
        cells = np.float32(rows * cols * n_row * n_col)
        vmem = pl.BlockSpec(memory_space=pltpu.VMEM)
        current, dual, tau = pl.pallas_call(
            functools.partial(kernel, n_row, n_col, cells),
            out_shape=(
                jax.ShapeDtypeStruct((rows, cols), f32),
                jax.ShapeDtypeStruct((2, rows, cols), f32),
                jax.ShapeDtypeStruct((1, LANE), f32),
            ),
            in_specs=[pl.BlockSpec(memory_space=pl.ANY)] * 2,
            out_specs=(vmem, vmem, vmem),
            scratch_shapes=[padded] * 10
            + [
                pltpu.VMEM((LANE, rows), f32),
                pltpu.VMEM((LANE, rows + 2 * LANE), f32),
                pltpu.VMEM((ITERS, n_row * n_col, 2, LANE), f32),
                pltpu.SemaphoreType.DMA((2,)),
                pltpu.SemaphoreType.DMA((10,)),
                pltpu.SemaphoreType.DMA((10,)),
                pltpu.SemaphoreType.DMA((ITERS,)),
                pltpu.SemaphoreType.DMA((ITERS,)),
            ],
            compiler_params=pltpu.CompilerParams(
                collective_id=0, has_side_effects=True, vmem_limit_bytes=40 * 1024 * 1024
            ),
        )(*(pltpu.with_memory_space_constraint(x, pltpu.HBM) for x in (noisy, fidelity)))
        return current, dual, tau[0, 0]

    return jax.shard_map(
        on_device,
        mesh=mesh,
        in_specs=(P("row", "col"), P("row", "col")),
        out_specs=(P("row", "col"), P(None, "row", "col"), P()),
        check_vma=False,
    )
```

```python
import functools
import jax
import jax.numpy as jnp
import numpy as np
from jax import lax
from jax.experimental import pallas as pl
from jax.experimental.pallas import tpu as pltpu
from jax.sharding import PartitionSpec as P

ITERS = 4
MESH = pl.DeviceIdType.MESH

first_tau = np.float32(0.35)
step_product = np.float32(0.124)
adapt_rate = 0.5
adapt_decay = 0.9
epsilon = np.float32(1e-06)

SUB = 8
LANE = 128
UNROLL = 5


def kernel(
    n_row, n_col, cells,
    noisy_hbm, fid_hbm,
    u_out, dual_out, tau_out,
    N, F, U, H, UB, PX, PY, GX, GY, DV, QT, CB, rb,
    load_sem, halo_send, halo_recv, red_send, red_recv, known,
):
    rows, cols = noisy_hbm.shape
    strips = rows // SUB + 2
    tiles = cols // LANE
    my_row, my_col = lax.axis_index("row"), lax.axis_index("col")
    f32 = jnp.float32

    def distance(ab):
        a, b = ab
        return sum(min(v % 4, 4 - v % 4) for v in (a // 2, b // 4, b % 4))

    def row_at(d):
        return lax.rem(my_row + d + n_row, n_row)

    def col_at(d):
        return lax.rem(my_col + d + n_col, n_col)

    sub = lax.broadcasted_iota(jnp.int32, (SUB, LANE), 0)
    lane = lax.broadcasted_iota(jnp.int32, (SUB, LANE), 1)
    sub_first, sub_last = sub == 0, sub == SUB - 1
    lane_first, lane_last = lane == 0, lane == LANE - 1

    def at(s, c):
        start = s * SUB if isinstance(s, int) else pl.multiple_of(s * SUB, SUB)
        return pl.ds(start, SUB), slice(c * LANE, (c + 1) * LANE)

    at_left, at_right = my_col == 0, my_col == n_col - 1
    last_col = jnp.logical_and(at_right, lane_last)
    outside = jnp.logical_and(at_left, lane >= LANE // 2)
    in_first_row = jnp.logical_and(my_row == 0, sub_first)

    def gradient_strip(field, s, which):
        cell = my_row * rows + (s - 1) * SUB + sub
        inside = jnp.logical_and(cell >= 0, cell < n_row * rows - 1)
        after = min(s + 1, strips - 1) if isinstance(s, int) else jnp.minimum(s + 1, strips - 1)
        here = {c: field[at(s, c)] for c in {c for w in which for c in (w, (w + 1) % (tiles + 1))}}
        turned = {c: pltpu.roll(h, LANE - 1, axis=1) for c, h in here.items()}
        for c in which:
            below = jnp.where(
                sub_last,
                pltpu.roll(field[at(after, c)], SUB - 1, axis=0),
                pltpu.roll(here[c], SUB - 1, axis=0),
            )
            right = jnp.where(lane_last, turned[(c + 1) % (tiles + 1)], turned[c])
            gx = jnp.where(inside, below - here[c], 0.0)
            gy = right - here[c]
            if c == tiles - 1:
                gy = jnp.where(last_col, 0.0, gy)
            if c == tiles:
                gy = jnp.where(outside, 0.0, gy)
            GX[at(s, c)] = gx
            GY[at(s, c)] = gy

    everywhere = tuple(range(tiles + 1))

    def between(s, carry):
        gradient_strip(UB, s, everywhere)
        for c in everywhere:
            H[at(s, c)] = F[at(s, c)] * (U[at(s, c)] - N[at(s, c)])
        return carry

    CB[...] = jnp.zeros_like(CB)

    own = slice(SUB, SUB + rows)
    edges, inner = [], []
    for i, (src, dst) in enumerate(((noisy_hbm, N), (fid_hbm, F))):
        for j, (part, group) in enumerate((
            (slice(0, LANE), edges), (slice(cols - LANE, cols), edges), (slice(LANE, cols - LANE), inner),
        )):
            group.append(pltpu.make_async_copy(src.at[:, part], dst.at[own, part], load_sem.at[i, j]))
    for load in edges + inner:
        load.start()

    around = [(a, b) for a in (-1, 0, 1) for b in (-1, 0, 1) if a or b]
    barrier = pltpu.get_barrier_semaphore()
    for a, b in around:
        pl.semaphore_signal(barrier, inc=1, device_id=(row_at(a), col_at(b)), device_id_type=MESH)

    rounds = [
        around,
        [(2 * a, 2 * b) for a, b in around],
        [(0, -4), (0, 4)],
    ]

    def tell(i):
        for a, b in rounds[i]:
            pl.semaphore_signal(known.at[i], inc=1, device_id=(row_at(a), col_at(b)), device_id_type=MESH)

    def learn(i):
        pl.semaphore_wait(known.at[i], len(rounds[i]))

    def pack(b):
        at = pl.ds(SUB + b * LANE, LANE)
        lanes = lax.broadcasted_iota(jnp.int32, (LANE, LANE), 1)
        n0, n7 = N[at, 0:LANE], N[at, cols - LANE : cols]
        f0 = pltpu.roll(F[at, 0:LANE], 8, axis=1)
        f7 = pltpu.roll(F[at, cols - LANE : cols], LANE - 8, axis=1)
        low = jnp.where(lanes < 8, n0, f0)
        high = jnp.where(lanes >= LANE - 8, n7, f7)
        return jnp.where(lanes < LANE // 2, low, high).T

    low, high = slice(0, 16), slice(LANE - 16, LANE)
    mid = slice(LANE, LANE + rows)
    top, bottom = slice(0, LANE), slice(LANE + rows, 2 * LANE + rows)
    first, last = slice(0, LANE), slice(rows - LANE, rows)
    below_rows = slice(rows + SUB, rows + 2 * SUB)
    moves = []
    for src, dst in ((noisy_hbm, N), (fid_hbm, F)):
        moves.append((src.at[0:SUB, :], dst.at[below_rows, 0:cols], -1, 0))
        moves.append((src.at[rows - SUB : rows, :], dst.at[0:SUB, 0:cols], 1, 0))
    moves.append((QT.at[low, :], CB.at[low, mid], 0, -1))
    moves.append((QT.at[high, :], CB.at[high, mid], 0, 1))
    for side, step in ((low, -1), (high, 1)):
        moves.append((QT.at[side, last], CB.at[side, top], 1, step))
        moves.append((QT.at[side, first], CB.at[side, bottom], -1, step))
    halos = [
        pltpu.make_async_remote_copy(
            src_ref=src, dst_ref=dst, send_sem=halo_send.at[i], recv_sem=halo_recv.at[i],
            device_id=(row_at(a), col_at(b)), device_id_type=MESH,
        )
        for i, (src, dst, a, b) in enumerate(moves)
    ]
    pl.semaphore_wait(barrier, len(around))
    for halo in halos[:4]:
        halo.start()
    for load in edges:
        load.wait()
    for b in range(rows // LANE):
        QT[:, b * LANE : (b + 1) * LANE] = pack(b)
    for halo in halos[4:]:
        halo.start()
    tell(0)
    for load in inner:
        load.wait()

    def interior(s, carry):
        gradient_strip(N, s, everywhere[: tiles - 1])
        return carry

    lax.fori_loop(1, strips - 2, interior, 0)

    for halo in halos:
        halo.wait_recv()
    learn(0)
    tell(1)

    def unpack(block, start, count, to):
        turned = block.T[start : start + count, :]
        lanes = lax.broadcasted_iota(jnp.int32, turned.shape, 1)
        edge = jnp.logical_or(lanes < 8, lanes >= LANE - 8)
        fid = jnp.where(
            lanes < LANE // 2, pltpu.roll(turned, LANE - 8, axis=1), pltpu.roll(turned, 8, axis=1)
        )
        N[to : to + count, cols : cols + LANE] = jnp.where(edge, turned, 0.0)
        F[to : to + count, cols : cols + LANE] = jnp.where(edge, fid, 1.0)

    unpack(CB[:, top], LANE - SUB, SUB, 0)
    for b in range(rows // LANE):
        unpack(CB[:, (b + 1) * LANE : (b + 2) * LANE], 0, LANE, SUB + b * LANE)
    unpack(CB[:, bottom], 0, SUB, SUB + rows)

    def border(s, carry):
        gradient_strip(N, s, everywhere[tiles - 1 :])
        return carry

    lax.fori_loop(1, strips - 2, border, 0)
    for s in (0, strips - 2, strips - 1):
        gradient_strip(N, s, everywhere)

    def strip(k, s, carry, counted, tau, sigma, itau, isigma):
        prev_x, prev_w, acc_p, acc_d, acc_l = carry
        prev_x, prev_w = list(prev_x), list(prev_w)
        final = k == ITERS - 1
        first_strip = isinstance(s, int) and s == 1

        def dual_step(c):
            qx, qy = sigma * GX[at(s, c)], sigma * GY[at(s, c)]
            if k:
                px, py = PX[at(s, c)], PY[at(s, c)]
                qx, qy = px + qx, py + qy
            scale = lax.rsqrt(jnp.maximum(qx * qx + qy * qy, 1.0))
            nx, ny = qx * scale, qy * scale
            tx, ty = (px - nx, py - ny) if k else (-nx, -ny)
            return nx, ny, tx, ty, pltpu.roll(nx, 1, axis=0), pltpu.roll(ny, 1, axis=1)

        def primal_step(c, dual, left):
            nx, ny, tx, ty, rx, ry = dual
            div = (nx - jnp.where(sub_first, prev_x[c], rx)) + (ny - jnp.where(lane_first, left, ry))
            prev_x[c] = rx
            if k:
                old = U[at(s, c)]
                du = (H[at(s, c)] - div) / (itau + F[at(s, c)])
            else:
                old = N[at(s, c)]
                du = div / (-itau - F[at(s, c)])
            new = old - du
            scaled = sigma * du
            wx, wy = tx + scaled, ty + scaled
            before = DV[at(s, c)] if k and counted and c < tiles else None
            if not final:
                PX[at(s, c)] = nx
                PY[at(s, c)] = ny
                U[at(s, c)] = new
                UB[at(s, c)] = new - du
                if c < tiles:
                    DV[at(s, c)] = div
            elif counted and c < tiles:
                own = at(s - 1, c)
                u_out[own] = new
                dual_out[(0, *own)] = nx
                dual_out[(1, *own)] = ny
            rwx, rwy = pltpu.roll(wx, 1, axis=0), pltpu.roll(wy, 1, axis=1)
            upper = prev_w[c]
            prev_w[c] = rwx
            return div, du, scaled, before, upper, rwx, rwy

        def residual(got, left):
            div, du, scaled, before, upper, rwx, rwy = got
            primal = du * itau - div
            if before is not None:
                primal = primal + before
            return (
                jnp.abs(primal),
                jnp.abs(jnp.where(sub_first, upper, rwx) - scaled),
                jnp.abs(jnp.where(lane_first, left, rwy) - scaled),
            )

        before_last = dual_step(tiles - 1)
        halo = dual_step(tiles)
        halo_got = primal_step(tiles, halo, before_last[5])
        left, left_w = halo[5], halo_got[6]
        for c in range(tiles):
            dual = before_last if c == tiles - 1 else dual_step(c)
            got = primal_step(c, dual, left)
            if counted:
                primal, along, across = residual(got, left_w)
                if first_strip:
                    along = jnp.where(in_first_row, 0.0, along)
                acc_p = acc_p + primal
                if c == 0:
                    acc_l = acc_l + across
                    acc_d = acc_d + along
                else:
                    acc_d = acc_d + (along + across)
            left, left_w = dual[5], got[6]
        return tuple(prev_x), tuple(prev_w), acc_p, acc_d, acc_l

    offsets = [(a, b) for a in range(n_row) for b in range(n_col) if a or b]
    offsets.sort(key=lambda ab: -distance(ab))
    partners = [(row_at(a), col_at(b)) for a, b in offsets]
    me = my_row * n_col + my_col
    others = len(offsets)

    def reduce_start(k, primal, dual):
        rb[k, me, 0:1, :] = jnp.sum(primal, axis=0, keepdims=True)
        rb[k, me, 1:2, :] = jnp.sum(dual, axis=0, keepdims=True)
        for partner in partners:
            pltpu.make_async_remote_copy(
                src_ref=rb.at[k, me], dst_ref=rb.at[k, me],
                send_sem=red_send.at[k], recv_sem=red_recv.at[k],
                device_id=partner, device_id_type=MESH,
            ).start()

    def reduce_end(k):
        got = rb.at[k, 0:others]
        pltpu.make_async_copy(got, got, red_recv.at[k]).wait()
        parts = [rb[k, i] for i in range(others + 1)]
        while len(parts) > 1:
            parts = [a + b for a, b in zip(parts[::2], parts[1::2])]
        total = jnp.sum(parts[0], axis=1, keepdims=True)
        return total[0:1], total[1:2]

    zero = jnp.zeros((SUB, LANE), f32)
    tau_one = jnp.full((1, 1), first_tau, f32)
    sigma_one = jnp.full((1, 1), step_product / first_tau, f32)
    for k in range(ITERS):
        def full(x):
            return jnp.broadcast_to(x, (SUB, LANE))

        steps = (full(tau_one), full(sigma_one), full(1.0 / tau_one), full(1.0 / sigma_one))
        none = (zero,) * (tiles + 1)
        carry = strip(k, 0, (none, none, zero, zero, zero), False, *steps)
        carry = strip(k, 1, carry, True, *steps)

        def body(i, carry, k=k, steps=steps):
            for j in range(UNROLL):
                carry = strip(k, 2 + i * UNROLL + j, carry, True, *steps)
            return carry

        whole = (strips - 3) // UNROLL
        if k == 0:
            carry = lax.fori_loop(0, whole // 2, body, carry)
            learn(1)
            tell(2)
            carry = lax.fori_loop(whole // 2, whole, body, carry)
            learn(2)
        else:
            carry = lax.fori_loop(0, whole, body, carry)
        for s in range(2 + whole * UNROLL, strips - 1):
            carry = strip(k, s, carry, True, *steps)
        if k < ITERS - 1:
            carry = strip(k, strips - 1, carry, False, *steps)
        _, _, primal, dual, at_first = carry
        dual = dual + jnp.where(jnp.logical_and(at_left, lane_first), 0.0, at_first)
        reduce_start(k, primal, dual * steps[3])
        if k < ITERS - 1:
            lax.fori_loop(0, strips, between, 0)
        primal, dual = reduce_end(k)
        ratio = jnp.log((primal / cells + epsilon) / (dual / cells + epsilon))
        rate = np.float32(adapt_rate * adapt_decay**k)
        tau_one = tau_one * jnp.exp(rate * ratio / (1.0 + jnp.abs(ratio)))
        sigma_one = step_product / tau_one
    tau_out[...] = jnp.broadcast_to(tau_one, tau_out.shape)

    for halo in halos:
        halo.wait_send()
    for k in range(ITERS):
        sent = rb.at[k, 0:others]
        pltpu.make_async_copy(sent, sent, red_send.at[k]).wait()


def solution(mesh):
    n_row, n_col = mesh.shape["row"], mesh.shape["col"]

    def on_device(noisy, fidelity):
        rows, cols = noisy.shape
        f32 = jnp.float32
        padded = pltpu.VMEM((rows + 2 * SUB, cols + LANE), f32)
        cells = np.float32(rows * cols * n_row * n_col)
        vmem = pl.BlockSpec(memory_space=pltpu.VMEM)
        current, dual, tau = pl.pallas_call(
            functools.partial(kernel, n_row, n_col, cells),
            out_shape=(
                jax.ShapeDtypeStruct((rows, cols), f32),
                jax.ShapeDtypeStruct((2, rows, cols), f32),
                jax.ShapeDtypeStruct((1, LANE), f32),
            ),
            in_specs=[pl.BlockSpec(memory_space=pl.ANY)] * 2,
            out_specs=(vmem, vmem, vmem),
            scratch_shapes=[padded] * 10
            + [
                pltpu.VMEM((LANE, rows), f32),
                pltpu.VMEM((LANE, rows + 2 * LANE), f32),
                pltpu.VMEM((ITERS, n_row * n_col, 2, LANE), f32),
                pltpu.SemaphoreType.DMA((2, 3)),
                pltpu.SemaphoreType.DMA((10,)),
                pltpu.SemaphoreType.DMA((10,)),
                pltpu.SemaphoreType.DMA((ITERS,)),
                pltpu.SemaphoreType.DMA((ITERS,)),
                pltpu.SemaphoreType.REGULAR((3,)),
            ],
            compiler_params=pltpu.CompilerParams(
                collective_id=0, has_side_effects=True, vmem_limit_bytes=40 * 1024 * 1024
            ),
        )(*(pltpu.with_memory_space_constraint(x, pltpu.HBM) for x in (noisy, fidelity)))
        return current, dual, tau[0, 0]

    return jax.shard_map(
        on_device,
        mesh=mesh,
        in_specs=(P("row", "col"), P("row", "col")),
        out_specs=(P("row", "col"), P(None, "row", "col"), P()),
        check_vma=False,
    )
```

```python
import functools
import jax
import jax.numpy as jnp
import numpy as np
from jax import lax
from jax.experimental import pallas as pl
from jax.experimental.pallas import tpu as pltpu
from jax.sharding import PartitionSpec as P

ITERS = 4
SIDE = 4
MESH = pl.DeviceIdType.MESH

first_tau = np.float32(0.35)
step_product = np.float32(0.124)
adapt_rate = 0.5
adapt_decay = 0.9
epsilon = np.float32(1e-06)

SUB = 8
LANE = 128
UNROLL = 6


def kernel(
    n_row, n_col, cells,
    noisy_hbm, fid_hbm,
    u_out, dual_out, tau_out,
    N, F, U, H, UB, DU, PX, PY, GX, GY, DV, QT, CB, rb,
    load_sem, halo_send, halo_recv, red_send, red_recv, known,
):
    rows, cols = noisy_hbm.shape
    strips = rows // SUB + 2
    tiles = cols // LANE
    my_row, my_col = lax.axis_index("row"), lax.axis_index("col")
    f32 = jnp.float32

    def distance(ab):
        a, b = ab
        return sum(min(v % 4, 4 - v % 4) for v in (a // 2, b // 4, b % 4))

    def row_at(d):
        return lax.rem(my_row + d + n_row, n_row)

    def col_at(d):
        return lax.rem(my_col + d + n_col, n_col)

    sub = lax.broadcasted_iota(jnp.int32, (SUB, LANE), 0)
    lane = lax.broadcasted_iota(jnp.int32, (SUB, LANE), 1)
    sub_first, sub_last = sub == 0, sub == SUB - 1
    lane_first, lane_last = lane == 0, lane == LANE - 1

    def at(s, c):
        start = s * SUB if isinstance(s, int) else pl.multiple_of(s * SUB, SUB)
        return pl.ds(start, SUB), slice(c * LANE, (c + 1) * LANE)

    at_left, at_right = my_col == 0, my_col == n_col - 1
    last_col = jnp.logical_and(at_right, lane_last)
    outside = jnp.logical_and(at_left, lane >= LANE // 2)
    in_first_row = jnp.logical_and(my_row == 0, sub_first)

    def gradient_strip(field, s, which):
        cell = my_row * rows + (s - 1) * SUB + sub
        inside = jnp.logical_and(cell >= 0, cell < n_row * rows - 1)
        after = min(s + 1, strips - 1) if isinstance(s, int) else jnp.minimum(s + 1, strips - 1)
        here = {c: field[at(s, c)] for c in {c for w in which for c in (w, (w + 1) % (tiles + 1))}}
        turned = {c: pltpu.roll(h, LANE - 1, axis=1) for c, h in here.items()}
        for c in which:
            below = jnp.where(
                sub_last,
                pltpu.roll(field[at(after, c)], SUB - 1, axis=0),
                pltpu.roll(here[c], SUB - 1, axis=0),
            )
            right = jnp.where(lane_last, turned[(c + 1) % (tiles + 1)], turned[c])
            gx = jnp.where(inside, below - here[c], 0.0)
            gy = right - here[c]
            if c == tiles - 1:
                gy = jnp.where(last_col, 0.0, gy)
            if c == tiles:
                gy = jnp.where(outside, 0.0, gy)
            GX[at(s, c)] = gx
            GY[at(s, c)] = gy

    everywhere = tuple(range(tiles + 1))

    def over_strips(first, end, group, work):
        def body(i, carry):
            for j in range(group):
                work(first + i * group + j)
            return carry

        trips = (end - first) // group
        if trips:
            lax.fori_loop(0, trips, body, 0)
        for s in range(first + trips * group, end):
            work(s)

    def between(k):
        def advance(s):
            for c in everywhere:
                du, noisy = DU[at(s, c)], N[at(s, c)]
                new = (U[at(s, c)] if k else noisy) - du
                U[at(s, c)] = new
                UB[at(s, c)] = new - du
                H[at(s, c)] = F[at(s, c)] * (new - noisy)

        over_strips(0, strips, 2, advance)
        over_strips(0, strips, 4, lambda s: gradient_strip(UB, s, everywhere))

    CB[...] = jnp.zeros_like(CB)

    own = slice(SUB, SUB + rows)
    edges, inner = [], []
    for i, (src, dst) in enumerate(((noisy_hbm, N), (fid_hbm, F))):
        for j, (part, group) in enumerate((
            (slice(0, LANE), edges), (slice(cols - LANE, cols), edges), (slice(LANE, cols - LANE), inner),
        )):
            group.append(pltpu.make_async_copy(src.at[:, part], dst.at[own, part], load_sem.at[i, j]))
    for load in edges + inner:
        load.start()

    def chip_at(y, core, z, x):
        row = lax.rem(my_row // 2 + y + SIDE, SIDE) * 2 + lax.rem(my_row + core, 2)
        col = lax.rem(my_col // SIDE + z + SIDE, SIDE) * SIDE + lax.rem(my_col + x + SIDE, SIDE)
        return row, col

    near = (-1, 0, 1)
    around = [(y, c, z, x) for y in near for c in (0, 1) for z in near for x in near if y or c or z or x]
    around.sort(key=lambda at: -sum(abs(v) for v in at))
    barrier = pltpu.get_barrier_semaphore()
    for where in around:
        pl.semaphore_signal(barrier, inc=1, device_id=chip_at(*where), device_id_type=MESH)

    corners = [(y, 0, z, x) for y in (-1, 1) for z in (-1, 1) for x in (-1, 1)]

    def tell():
        for where in corners:
            pl.semaphore_signal(known, inc=1, device_id=chip_at(*where), device_id_type=MESH)

    def pack(b):
        at = pl.ds(SUB + b * LANE, LANE)
        lanes = lax.broadcasted_iota(jnp.int32, (LANE, LANE), 1)
        n0, n7 = N[at, 0:LANE], N[at, cols - LANE : cols]
        f0 = pltpu.roll(F[at, 0:LANE], 8, axis=1)
        f7 = pltpu.roll(F[at, cols - LANE : cols], LANE - 8, axis=1)
        low = jnp.where(lanes < 8, n0, f0)
        high = jnp.where(lanes >= LANE - 8, n7, f7)
        return jnp.where(lanes < LANE // 2, low, high).T

    low, high = slice(0, 16), slice(LANE - 16, LANE)
    mid = slice(LANE, LANE + rows)
    top, bottom = slice(0, LANE), slice(LANE + rows, 2 * LANE + rows)
    first, last = slice(0, LANE), slice(rows - LANE, rows)
    below_rows = slice(rows + SUB, rows + 2 * SUB)
    moves = []
    for src, dst in ((noisy_hbm, N), (fid_hbm, F)):
        moves.append((src.at[0:SUB, :], dst.at[below_rows, 0:cols], -1, 0))
        moves.append((src.at[rows - SUB : rows, :], dst.at[0:SUB, 0:cols], 1, 0))
    moves.append((QT.at[low, :], CB.at[low, mid], 0, -1))
    moves.append((QT.at[high, :], CB.at[high, mid], 0, 1))
    for side, step in ((low, -1), (high, 1)):
        moves.append((QT.at[side, last], CB.at[side, top], 1, step))
        moves.append((QT.at[side, first], CB.at[side, bottom], -1, step))
    halos = [
        pltpu.make_async_remote_copy(
            src_ref=src, dst_ref=dst, send_sem=halo_send.at[i], recv_sem=halo_recv.at[i],
            device_id=(row_at(a), col_at(b)), device_id_type=MESH,
        )
        for i, (src, dst, a, b) in enumerate(moves)
    ]
    pl.semaphore_wait(barrier, len(around))
    tell()
    for halo in halos[:4]:
        halo.start()
    for load in edges:
        load.wait()
    for b in range(rows // LANE):
        QT[:, b * LANE : (b + 1) * LANE] = pack(b)
    for halo in halos[4:]:
        halo.start()
    for load in inner:
        load.wait()

    over_strips(1, strips - 2, 4, lambda s: gradient_strip(N, s, everywhere[: tiles - 1]))

    for halo in halos:
        halo.wait_recv()

    def unpack(block, start, count, to):
        turned = block.T[start : start + count, :]
        lanes = lax.broadcasted_iota(jnp.int32, turned.shape, 1)
        edge = jnp.logical_or(lanes < 8, lanes >= LANE - 8)
        fid = jnp.where(
            lanes < LANE // 2, pltpu.roll(turned, LANE - 8, axis=1), pltpu.roll(turned, 8, axis=1)
        )
        N[to : to + count, cols : cols + LANE] = jnp.where(edge, turned, 0.0)
        F[to : to + count, cols : cols + LANE] = jnp.where(edge, fid, 1.0)

    unpack(CB[:, top], LANE - SUB, SUB, 0)
    for b in range(rows // LANE):
        unpack(CB[:, (b + 1) * LANE : (b + 2) * LANE], 0, LANE, SUB + b * LANE)
    unpack(CB[:, bottom], 0, SUB, SUB + rows)

    over_strips(1, strips - 2, 16, lambda s: gradient_strip(N, s, everywhere[tiles - 1 :]))
    for s in (0, strips - 2, strips - 1):
        gradient_strip(N, s, everywhere)

    def strip(k, s, carry, counted, tau, sigma, itau, isigma):
        prev_x, prev_w, acc_p, acc_d, acc_l = carry
        prev_x, prev_w = list(prev_x), list(prev_w)
        final = k == ITERS - 1
        first_strip = isinstance(s, int) and s == 1

        def dual_step(c):
            qx, qy = sigma * GX[at(s, c)], sigma * GY[at(s, c)]
            if k:
                px, py = PX[at(s, c)], PY[at(s, c)]
                qx, qy = px + qx, py + qy
            scale = lax.rsqrt(jnp.maximum(qx * qx + qy * qy, 1.0))
            nx, ny = qx * scale, qy * scale
            tx, ty = (px - nx, py - ny) if k else (-nx, -ny)
            return nx, ny, tx, ty, pltpu.roll(nx, 1, axis=0), pltpu.roll(ny, 1, axis=1)

        def primal_step(c, dual, left):
            nx, ny, tx, ty, rx, ry = dual
            div = (nx - jnp.where(sub_first, prev_x[c], rx)) + (ny - jnp.where(lane_first, left, ry))
            prev_x[c] = rx
            if k:
                du = (H[at(s, c)] - div) / (itau + F[at(s, c)])
            else:
                du = div / (-itau - F[at(s, c)])
            DU[at(s, c)] = du
            scaled = sigma * du
            wx, wy = tx + scaled, ty + scaled
            before = DV[at(s, c)] if k and counted and c < tiles else None
            if not final:
                PX[at(s, c)] = nx
                PY[at(s, c)] = ny
                if c < tiles:
                    DV[at(s, c)] = div
            elif counted and c < tiles:
                own = at(s - 1, c)
                dual_out[(0, *own)] = nx
                dual_out[(1, *own)] = ny
            rwx, rwy = pltpu.roll(wx, 1, axis=0), pltpu.roll(wy, 1, axis=1)
            upper = prev_w[c]
            prev_w[c] = rwx
            return div, du, scaled, before, upper, rwx, rwy

        def residual(got, left):
            div, du, scaled, before, upper, rwx, rwy = got
            primal = du * itau - div
            if before is not None:
                primal = primal + before
            return (
                jnp.abs(primal),
                jnp.abs(jnp.where(sub_first, upper, rwx) - scaled),
                jnp.abs(jnp.where(lane_first, left, rwy) - scaled),
            )

        before_last = dual_step(tiles - 1)
        halo = dual_step(tiles)
        halo_got = primal_step(tiles, halo, before_last[5])
        left, left_w = halo[5], halo_got[6]
        for c in range(tiles):
            dual = before_last if c == tiles - 1 else dual_step(c)
            got = primal_step(c, dual, left)
            if counted:
                primal, along, across = residual(got, left_w)
                if first_strip:
                    along = jnp.where(in_first_row, 0.0, along)
                acc_p = acc_p + primal
                if c == 0:
                    acc_l = acc_l + across
                    acc_d = acc_d + along
                else:
                    acc_d = acc_d + (along + across)
            left, left_w = dual[5], got[6]
        return tuple(prev_x), tuple(prev_w), acc_p, acc_d, acc_l

    offsets = [(a, b) for a in range(n_row) for b in range(n_col) if a or b]
    offsets.sort(key=lambda ab: -distance(ab))
    partners = [(row_at(a), col_at(b)) for a, b in offsets]
    me = my_row * n_col + my_col
    others = len(offsets)

    def reduce_start(k, primal, dual):
        rb[k, me, 0:1, :] = jnp.sum(primal, axis=0, keepdims=True)
        rb[k, me, 1:2, :] = jnp.sum(dual, axis=0, keepdims=True)
        for partner in partners:
            pltpu.make_async_remote_copy(
                src_ref=rb.at[k, me], dst_ref=rb.at[k, me],
                send_sem=red_send.at[k], recv_sem=red_recv.at[k],
                device_id=partner, device_id_type=MESH,
            ).start()

    def reduce_end(k):
        got = rb.at[k, 0:others]
        pltpu.make_async_copy(got, got, red_recv.at[k]).wait()
        parts = [rb[k, i] for i in range(others + 1)]
        while len(parts) > 1:
            parts = [a + b for a, b in zip(parts[::2], parts[1::2])]
        total = jnp.sum(parts[0], axis=1, keepdims=True)
        return total[0:1], total[1:2]

    def finish(s):
        for c in range(tiles):
            u_out[at(s - 1, c)] = U[at(s, c)] - DU[at(s, c)]

    zero = jnp.zeros((SUB, LANE), f32)
    tau_one = jnp.full((1, 1), first_tau, f32)
    sigma_one = jnp.full((1, 1), step_product / first_tau, f32)
    for k in range(ITERS):
        def full(x):
            return jnp.broadcast_to(x, (SUB, LANE))

        steps = (full(tau_one), full(sigma_one), full(1.0 / tau_one), full(1.0 / sigma_one))
        none = (zero,) * (tiles + 1)
        carry = strip(k, 0, (none, none, zero, zero, zero), False, *steps)
        carry = strip(k, 1, carry, True, *steps)

        def body(i, carry, k=k, steps=steps):
            for j in range(UNROLL):
                carry = strip(k, 2 + i * UNROLL + j, carry, True, *steps)
            return carry

        whole = (strips - 3) // UNROLL
        carry = lax.fori_loop(0, whole, body, carry)
        for s in range(2 + whole * UNROLL, strips - 1):
            carry = strip(k, s, carry, True, *steps)
        _, _, primal, dual, at_first = carry
        dual = dual + jnp.where(jnp.logical_and(at_left, lane_first), 0.0, at_first)
        if k == 0:
            pl.semaphore_wait(known, len(corners))
        reduce_start(k, primal, dual * steps[3])
        if k < ITERS - 1:
            strip(k, strips - 1, carry, False, *steps)
            between(k)
        else:
            over_strips(1, strips - 1, 4, finish)
        primal, dual = reduce_end(k)
        ratio = jnp.log((primal / cells + epsilon) / (dual / cells + epsilon))
        rate = np.float32(adapt_rate * adapt_decay**k)
        tau_one = tau_one * jnp.exp(rate * ratio / (1.0 + jnp.abs(ratio)))
        sigma_one = step_product / tau_one
    tau_out[...] = jnp.broadcast_to(tau_one, tau_out.shape)

    for halo in halos:
        halo.wait_send()
    for k in range(ITERS):
        sent = rb.at[k, 0:others]
        pltpu.make_async_copy(sent, sent, red_send.at[k]).wait()


def solution(mesh):
    n_row, n_col = mesh.shape["row"], mesh.shape["col"]

    def on_device(noisy, fidelity):
        rows, cols = noisy.shape
        f32 = jnp.float32
        padded = pltpu.VMEM((rows + 2 * SUB, cols + LANE), f32)
        cells = np.float32(rows * cols * n_row * n_col)
        vmem = pl.BlockSpec(memory_space=pltpu.VMEM)
        current, dual, tau = pl.pallas_call(
            functools.partial(kernel, n_row, n_col, cells),
            out_shape=(
                jax.ShapeDtypeStruct((rows, cols), f32),
                jax.ShapeDtypeStruct((2, rows, cols), f32),
                jax.ShapeDtypeStruct((1, LANE), f32),
            ),
            in_specs=[pl.BlockSpec(memory_space=pl.ANY)] * 2,
            out_specs=(vmem, vmem, vmem),
            scratch_shapes=[padded] * 11
            + [
                pltpu.VMEM((LANE, rows), f32),
                pltpu.VMEM((LANE, rows + 2 * LANE), f32),
                pltpu.VMEM((ITERS, n_row * n_col, 2, LANE), f32),
                pltpu.SemaphoreType.DMA((2, 3)),
                pltpu.SemaphoreType.DMA((10,)),
                pltpu.SemaphoreType.DMA((10,)),
                pltpu.SemaphoreType.DMA((ITERS,)),
                pltpu.SemaphoreType.DMA((ITERS,)),
                pltpu.SemaphoreType.REGULAR,
            ],
            compiler_params=pltpu.CompilerParams(
                collective_id=0, has_side_effects=True, vmem_limit_bytes=40 * 1024 * 1024
            ),
        )(*(pltpu.with_memory_space_constraint(x, pltpu.HBM) for x in (noisy, fidelity)))
        return current, dual, tau[0, 0]

    return jax.shard_map(
        on_device,
        mesh=mesh,
        in_specs=(P("row", "col"), P("row", "col")),
        out_specs=(P("row", "col"), P(None, "row", "col"), P()),
        check_vma=False,
    )
```

```python
import functools
import jax
import jax.numpy as jnp
import numpy as np
from jax import lax
from jax.experimental import pallas as pl
from jax.experimental.pallas import tpu as pltpu
from jax.sharding import PartitionSpec as P

ITERS = 4
SIDE = 4
MESH = pl.DeviceIdType.MESH

first_tau = np.float32(0.35)
step_product = np.float32(0.124)
adapt_rate = 0.5
adapt_decay = 0.9
epsilon = np.float32(1e-06)

SUB = 8
LANE = 128
UNROLL = 6


def kernel(
    n_row, n_col, cells,
    noisy_hbm, fid_hbm,
    u_out, dual_out, tau_out,
    N, F, U, H, UB, DU, PX, PY, GX, GY, DV, QT, CB, rb,
    load_sem, halo_send, halo_recv, red_send, red_recv, known,
):
    rows, cols = noisy_hbm.shape
    strips = rows // SUB + 2
    tiles = cols // LANE
    my_row, my_col = lax.axis_index("row"), lax.axis_index("col")
    f32 = jnp.float32

    def distance(ab):
        a, b = ab
        return sum(min(v % 4, 4 - v % 4) for v in (a // 2, b // 4, b % 4))

    def row_at(d):
        return lax.rem(my_row + d + n_row, n_row)

    def col_at(d):
        return lax.rem(my_col + d + n_col, n_col)

    sub = lax.broadcasted_iota(jnp.int32, (SUB, LANE), 0)
    lane = lax.broadcasted_iota(jnp.int32, (SUB, LANE), 1)
    sub_first, sub_last = sub == 0, sub == SUB - 1
    lane_first, lane_last = lane == 0, lane == LANE - 1

    def at(s, c):
        start = s * SUB if isinstance(s, int) else pl.multiple_of(s * SUB, SUB)
        return pl.ds(start, SUB), slice(c * LANE, (c + 1) * LANE)

    at_left, at_right = my_col == 0, my_col == n_col - 1
    last_col = jnp.logical_and(at_right, lane_last)
    outside = jnp.logical_and(at_left, lane >= LANE // 2)
    in_first_row = jnp.logical_and(my_row == 0, sub_first)

    def gradient_strip(field, s, which):
        cell = my_row * rows + (s - 1) * SUB + sub
        inside = jnp.logical_and(cell >= 0, cell < n_row * rows - 1)
        after = min(s + 1, strips - 1) if isinstance(s, int) else jnp.minimum(s + 1, strips - 1)
        here = {c: field[at(s, c)] for c in {c for w in which for c in (w, (w + 1) % (tiles + 1))}}
        turned = {c: pltpu.roll(h, LANE - 1, axis=1) for c, h in here.items()}
        for c in which:
            below = jnp.where(
                sub_last,
                pltpu.roll(field[at(after, c)], SUB - 1, axis=0),
                pltpu.roll(here[c], SUB - 1, axis=0),
            )
            right = jnp.where(lane_last, turned[(c + 1) % (tiles + 1)], turned[c])
            gx = jnp.where(inside, below - here[c], 0.0)
            gy = right - here[c]
            if c == tiles - 1:
                gy = jnp.where(last_col, 0.0, gy)
            if c == tiles:
                gy = jnp.where(outside, 0.0, gy)
            GX[at(s, c)] = gx
            GY[at(s, c)] = gy

    everywhere = tuple(range(tiles + 1))

    def over_strips(first, end, group, work):
        def body(i, carry):
            for j in range(group):
                work(first + i * group + j)
            return carry

        trips = (end - first) // group
        if trips:
            lax.fori_loop(0, trips, body, 0)
        for s in range(first + trips * group, end):
            work(s)

    def between(k):
        def advance(s):
            for c in everywhere:
                du, noisy = DU[at(s, c)], N[at(s, c)]
                new = (U[at(s, c)] if k else noisy) - du
                U[at(s, c)] = new
                UB[at(s, c)] = new - du
                H[at(s, c)] = F[at(s, c)] * (new - noisy)

        over_strips(0, strips, 2, advance)
        over_strips(0, strips, 4, lambda s: gradient_strip(UB, s, everywhere))

    own = slice(SUB, SUB + rows)
    edges, inner = [], []
    for i, (src, dst) in enumerate(((noisy_hbm, N), (fid_hbm, F))):
        for j, (part, group) in enumerate((
            (slice(0, LANE), edges), (slice(cols - LANE, cols), edges), (slice(LANE, cols - LANE), inner),
        )):
            group.append(pltpu.make_async_copy(src.at[:, part], dst.at[own, part], load_sem.at[i, j]))
    for load in edges + inner:
        load.start()

    CB[...] = jnp.zeros_like(CB)

    def chip_at(y, core, z, x):
        row = lax.rem(my_row // 2 + y + SIDE, SIDE) * 2 + lax.rem(my_row + core, 2)
        col = lax.rem(my_col // SIDE + z + SIDE, SIDE) * SIDE + lax.rem(my_col + x + SIDE, SIDE)
        return row, col

    near = (-1, 0, 1)
    around = [(y, c, z, x) for y in near for c in (0, 1) for z in near for x in near if y or c or z or x]
    around.sort(key=lambda at: -sum(abs(v) for v in at))
    barrier = pltpu.get_barrier_semaphore()
    for where in around:
        pl.semaphore_signal(barrier, inc=1, device_id=chip_at(*where), device_id_type=MESH)

    corners = [(y, 0, z, x) for y in (-1, 1) for z in (-1, 1) for x in (-1, 1)]

    def tell():
        for where in corners:
            pl.semaphore_signal(known, inc=1, device_id=chip_at(*where), device_id_type=MESH)

    def pack(b):
        at = pl.ds(SUB + b * LANE, LANE)
        lanes = lax.broadcasted_iota(jnp.int32, (LANE, LANE), 1)
        n0, n7 = N[at, 0:LANE], N[at, cols - LANE : cols]
        f0 = pltpu.roll(F[at, 0:LANE], 8, axis=1)
        f7 = pltpu.roll(F[at, cols - LANE : cols], LANE - 8, axis=1)
        low = jnp.where(lanes < 8, n0, f0)
        high = jnp.where(lanes >= LANE - 8, n7, f7)
        return jnp.where(lanes < LANE // 2, low, high).T

    low, high = slice(0, 16), slice(LANE - 16, LANE)
    mid = slice(LANE, LANE + rows)
    top, bottom = slice(0, LANE), slice(LANE + rows, 2 * LANE + rows)
    first, last = slice(0, LANE), slice(rows - LANE, rows)
    below_rows = slice(rows + SUB, rows + 2 * SUB)
    moves = []
    for src, dst in ((noisy_hbm, N), (fid_hbm, F)):
        moves.append((src.at[0:SUB, :], dst.at[below_rows, 0:cols], -1, 0))
        moves.append((src.at[rows - SUB : rows, :], dst.at[0:SUB, 0:cols], 1, 0))
    moves.append((QT.at[low, :], CB.at[low, mid], 0, -1))
    moves.append((QT.at[high, :], CB.at[high, mid], 0, 1))
    for side, step in ((low, -1), (high, 1)):
        moves.append((QT.at[side, last], CB.at[side, top], 1, step))
        moves.append((QT.at[side, first], CB.at[side, bottom], -1, step))
    halos = [
        pltpu.make_async_remote_copy(
            src_ref=src, dst_ref=dst, send_sem=halo_send.at[i], recv_sem=halo_recv.at[i],
            device_id=(row_at(a), col_at(b)), device_id_type=MESH,
        )
        for i, (src, dst, a, b) in enumerate(moves)
    ]
    pl.semaphore_wait(barrier, len(around))
    tell()
    for halo in halos[:4]:
        halo.start()
    for load in edges:
        load.wait()
    for b in range(rows // LANE):
        QT[:, b * LANE : (b + 1) * LANE] = pack(b)
    for halo in halos[4:]:
        halo.start()
    for load in inner:
        load.wait()

    over_strips(1, strips - 2, 4, lambda s: gradient_strip(N, s, everywhere[: tiles - 1]))

    for halo in halos:
        halo.wait_recv()

    def unpack(block, start, count, to):
        turned = block.T[start : start + count, :]
        lanes = lax.broadcasted_iota(jnp.int32, turned.shape, 1)
        edge = jnp.logical_or(lanes < 8, lanes >= LANE - 8)
        fid = jnp.where(
            lanes < LANE // 2, pltpu.roll(turned, LANE - 8, axis=1), pltpu.roll(turned, 8, axis=1)
        )
        N[to : to + count, cols : cols + LANE] = jnp.where(edge, turned, 0.0)
        F[to : to + count, cols : cols + LANE] = jnp.where(edge, fid, 1.0)

    unpack(CB[:, top], LANE - SUB, SUB, 0)
    for b in range(rows // LANE):
        unpack(CB[:, (b + 1) * LANE : (b + 2) * LANE], 0, LANE, SUB + b * LANE)
    unpack(CB[:, bottom], 0, SUB, SUB + rows)

    over_strips(1, strips - 2, 16, lambda s: gradient_strip(N, s, everywhere[tiles - 1 :]))
    for s in (0, strips - 2, strips - 1):
        gradient_strip(N, s, everywhere)

    def strip(k, s, carry, counted, tau, sigma, itau, isigma):
        prev_x, prev_w, acc_p, acc_d, acc_l = carry
        prev_x, prev_w = list(prev_x), list(prev_w)
        final = k == ITERS - 1
        first_strip = isinstance(s, int) and s == 1

        def dual_step(c):
            qx, qy = sigma * GX[at(s, c)], sigma * GY[at(s, c)]
            if k:
                px, py = PX[at(s, c)], PY[at(s, c)]
                qx, qy = px + qx, py + qy
            scale = lax.rsqrt(jnp.maximum(qx * qx + qy * qy, 1.0))
            nx, ny = qx * scale, qy * scale
            tx, ty = (px - nx, py - ny) if k else (-nx, -ny)
            return nx, ny, tx, ty, pltpu.roll(nx, 1, axis=0), pltpu.roll(ny, 1, axis=1)

        def primal_step(c, dual, left):
            nx, ny, tx, ty, rx, ry = dual
            div = (nx - jnp.where(sub_first, prev_x[c], rx)) + (ny - jnp.where(lane_first, left, ry))
            prev_x[c] = rx
            if k:
                du = (H[at(s, c)] - div) / (itau + F[at(s, c)])
            else:
                du = div / (-itau - F[at(s, c)])
            DU[at(s, c)] = du
            scaled = sigma * du
            wx, wy = tx + scaled, ty + scaled
            before = DV[at(s, c)] if k and counted and c < tiles else None
            if not final:
                PX[at(s, c)] = nx
                PY[at(s, c)] = ny
                if c < tiles:
                    DV[at(s, c)] = div
            elif counted and c < tiles:
                own = at(s - 1, c)
                dual_out[(0, *own)] = nx
                dual_out[(1, *own)] = ny
            rwx, rwy = pltpu.roll(wx, 1, axis=0), pltpu.roll(wy, 1, axis=1)
            upper = prev_w[c]
            prev_w[c] = rwx
            return div, du, scaled, before, upper, rwx, rwy

        def residual(got, left):
            div, du, scaled, before, upper, rwx, rwy = got
            primal = du * itau - div
            if before is not None:
                primal = primal + before
            return (
                jnp.abs(primal),
                jnp.abs(jnp.where(sub_first, upper, rwx) - scaled),
                jnp.abs(jnp.where(lane_first, left, rwy) - scaled),
            )

        before_last = dual_step(tiles - 1)
        halo = dual_step(tiles)
        halo_got = primal_step(tiles, halo, before_last[5])
        left, left_w = halo[5], halo_got[6]
        for c in range(tiles):
            dual = before_last if c == tiles - 1 else dual_step(c)
            got = primal_step(c, dual, left)
            if counted:
                primal, along, across = residual(got, left_w)
                if first_strip:
                    along = jnp.where(in_first_row, 0.0, along)
                acc_p = acc_p + primal
                if c == 0:
                    acc_l = acc_l + across
                    acc_d = acc_d + along
                else:
                    acc_d = acc_d + (along + across)
            left, left_w = dual[5], got[6]
        return tuple(prev_x), tuple(prev_w), acc_p, acc_d, acc_l

    offsets = [(a, b) for a in range(n_row) for b in range(n_col) if a or b]
    offsets.sort(key=lambda ab: -distance(ab))
    partners = [(row_at(a), col_at(b)) for a, b in offsets]
    me = my_row * n_col + my_col
    others = len(offsets)

    def reduce_start(k, primal, dual):
        half = LANE // 2
        both = jnp.where(lane < half, primal + pltpu.roll(primal, half, axis=1), dual + pltpu.roll(dual, half, axis=1))
        rb[k, me] = jnp.sum(both, axis=0, keepdims=True)
        for partner in partners:
            pltpu.make_async_remote_copy(
                src_ref=rb.at[k, me], dst_ref=rb.at[k, me],
                send_sem=red_send.at[k], recv_sem=red_recv.at[k],
                device_id=partner, device_id_type=MESH,
            ).start()

    def reduce_end(k):
        got = rb.at[k, 0:others]
        pltpu.make_async_copy(got, got, red_recv.at[k]).wait()
        parts = [rb[k, i] for i in range(others + 1)]
        while len(parts) > 1:
            parts = [a + b for a, b in zip(parts[::2], parts[1::2])]
        lower = lax.broadcasted_iota(jnp.int32, (1, LANE), 1) < LANE // 2
        primal = jnp.sum(jnp.where(lower, parts[0], 0.0), axis=1, keepdims=True)
        dual = jnp.sum(jnp.where(lower, 0.0, parts[0]), axis=1, keepdims=True)
        return primal, dual

    def finish(s):
        for c in range(tiles):
            u_out[at(s - 1, c)] = U[at(s, c)] - DU[at(s, c)]

    zero = jnp.zeros((SUB, LANE), f32)
    tau_one = jnp.full((1, 1), first_tau, f32)
    sigma_one = jnp.full((1, 1), step_product / first_tau, f32)
    for k in range(ITERS):
        def full(x):
            return jnp.broadcast_to(x, (SUB, LANE))

        steps = (full(tau_one), full(sigma_one), full(1.0 / tau_one), full(1.0 / sigma_one))
        none = (zero,) * (tiles + 1)
        carry = strip(k, 0, (none, none, zero, zero, zero), False, *steps)
        carry = strip(k, 1, carry, True, *steps)

        def body(i, carry, k=k, steps=steps):
            for j in range(UNROLL):
                carry = strip(k, 2 + i * UNROLL + j, carry, True, *steps)
            return carry

        whole = (strips - 3) // UNROLL
        carry = lax.fori_loop(0, whole, body, carry)
        for s in range(2 + whole * UNROLL, strips - 1):
            carry = strip(k, s, carry, True, *steps)
        _, _, primal, dual, at_first = carry
        dual = dual + jnp.where(jnp.logical_and(at_left, lane_first), 0.0, at_first)
        if k == 0:
            pl.semaphore_wait(known, len(corners))
        reduce_start(k, primal, dual * steps[3])
        if k < ITERS - 1:
            strip(k, strips - 1, carry, False, *steps)
            between(k)
        else:
            over_strips(1, strips - 1, 4, finish)
        primal, dual = reduce_end(k)
        ratio = jnp.log((primal / cells + epsilon) / (dual / cells + epsilon))
        rate = np.float32(adapt_rate * adapt_decay**k)
        tau_one = tau_one * jnp.exp(rate * ratio / (1.0 + jnp.abs(ratio)))
        sigma_one = step_product / tau_one
    tau_out[...] = jnp.broadcast_to(tau_one, tau_out.shape)

    for halo in halos:
        halo.wait_send()
    for k in range(ITERS):
        sent = rb.at[k, 0:others]
        pltpu.make_async_copy(sent, sent, red_send.at[k]).wait()


def write_kernel(u_ref, dual_ref, u_hbm, dual_hbm, sem):
    moves = [(u_ref, u_hbm), (dual_ref.at[0], dual_hbm.at[0]), (dual_ref.at[1], dual_hbm.at[1])]
    copies = [pltpu.make_async_copy(src, dst, sem.at[i]) for i, (src, dst) in enumerate(moves)]
    for copy in copies:
        copy.start()
    for copy in copies:
        copy.wait()


def written(current, dual):
    vmem, hbm = (pl.BlockSpec(memory_space=space) for space in (pltpu.VMEM, pltpu.HBM))
    return pl.pallas_call(
        write_kernel,
        out_shape=tuple(jax.ShapeDtypeStruct(x.shape, x.dtype) for x in (current, dual)),
        in_specs=[vmem, vmem],
        out_specs=(hbm, hbm),
        scratch_shapes=[pltpu.SemaphoreType.DMA((3,))],
        compiler_params=pltpu.CompilerParams(vmem_limit_bytes=8 * 1024 * 1024),
    )(current, dual)


def solution(mesh):
    n_row, n_col = mesh.shape["row"], mesh.shape["col"]

    def on_device(noisy, fidelity):
        rows, cols = noisy.shape
        f32 = jnp.float32
        padded = pltpu.VMEM((rows + 2 * SUB, cols + LANE), f32)
        cells = np.float32(rows * cols * n_row * n_col)
        vmem = pl.BlockSpec(memory_space=pltpu.VMEM)
        current, dual, tau = pl.pallas_call(
            functools.partial(kernel, n_row, n_col, cells),
            out_shape=(
                jax.ShapeDtypeStruct((rows, cols), f32),
                jax.ShapeDtypeStruct((2, rows, cols), f32),
                jax.ShapeDtypeStruct((1, LANE), f32),
            ),
            in_specs=[pl.BlockSpec(memory_space=pl.ANY)] * 2,
            out_specs=(vmem, vmem, vmem),
            scratch_shapes=[padded] * 11
            + [
                pltpu.VMEM((LANE, rows), f32),
                pltpu.VMEM((LANE, rows + 2 * LANE), f32),
                pltpu.VMEM((ITERS, n_row * n_col, 1, LANE), f32),
                pltpu.SemaphoreType.DMA((2, 3)),
                pltpu.SemaphoreType.DMA((10,)),
                pltpu.SemaphoreType.DMA((10,)),
                pltpu.SemaphoreType.DMA((ITERS,)),
                pltpu.SemaphoreType.DMA((ITERS,)),
                pltpu.SemaphoreType.REGULAR,
            ],
            compiler_params=pltpu.CompilerParams(
                collective_id=0, has_side_effects=True, vmem_limit_bytes=40 * 1024 * 1024
            ),
        )(*(pltpu.with_memory_space_constraint(x, pltpu.HBM) for x in (noisy, fidelity)))
        current, dual = written(current, dual)
        return current, dual, tau[0, 0]

    return jax.shard_map(
        on_device,
        mesh=mesh,
        in_specs=(P("row", "col"), P("row", "col")),
        out_specs=(P("row", "col"), P(None, "row", "col"), P()),
        check_vma=False,
    )
```

```python
import functools
import jax
import jax.numpy as jnp
import numpy as np
from jax import lax
from jax.experimental import pallas as pl
from jax.experimental.pallas import tpu as pltpu
from jax.sharding import PartitionSpec as P

ITERS = 4
SIDE = 4
MESH = pl.DeviceIdType.MESH

first_tau = np.float32(0.35)
step_product = np.float32(0.124)
adapt_rate = 0.5
adapt_decay = 0.9
epsilon = np.float32(1e-06)

SUB = 8
LANE = 128
UNROLL = 10


def kernel(
    n_row, n_col, cells,
    noisy_hbm, fid_hbm,
    u_out, dual_out, tau_out,
    N, F, U, H, UB, DU, PX, PY, GX, GY, DV, QT, CB, rb,
    load_sem, halo_send, halo_recv, red_send, red_recv, known,
):
    rows, cols = noisy_hbm.shape
    strips = rows // SUB + 2
    tiles = cols // LANE
    my_row, my_col = lax.axis_index("row"), lax.axis_index("col")
    f32 = jnp.float32

    def distance(ab):
        a, b = ab
        return sum(min(v % 4, 4 - v % 4) for v in (a // 2, b // 4, b % 4))

    def row_at(d):
        return lax.rem(my_row + d + n_row, n_row)

    def col_at(d):
        return lax.rem(my_col + d + n_col, n_col)

    sub = lax.broadcasted_iota(jnp.int32, (SUB, LANE), 0)
    lane = lax.broadcasted_iota(jnp.int32, (SUB, LANE), 1)
    sub_first, sub_last = sub == 0, sub == SUB - 1
    lane_first, lane_last = lane == 0, lane == LANE - 1

    def at(s, c):
        start = s * SUB if isinstance(s, int) else pl.multiple_of(s * SUB, SUB)
        return pl.ds(start, SUB), slice(c * LANE, (c + 1) * LANE)

    at_left, at_right = my_col == 0, my_col == n_col - 1
    last_col = jnp.logical_and(at_right, lane_last)
    outside = jnp.logical_and(at_left, lane >= LANE // 2)
    in_first_row = jnp.logical_and(my_row == 0, sub_first)

    def gradient_strip(field, s, which):
        cell = my_row * rows + (s - 1) * SUB + sub
        inside = jnp.logical_and(cell >= 0, cell < n_row * rows - 1)
        after = min(s + 1, strips - 1) if isinstance(s, int) else jnp.minimum(s + 1, strips - 1)
        here = {c: field[at(s, c)] for c in {c for w in which for c in (w, (w + 1) % (tiles + 1))}}
        turned = {c: pltpu.roll(h, LANE - 1, axis=1) for c, h in here.items()}
        for c in which:
            below = jnp.where(
                sub_last,
                pltpu.roll(field[at(after, c)], SUB - 1, axis=0),
                pltpu.roll(here[c], SUB - 1, axis=0),
            )
            right = jnp.where(lane_last, turned[(c + 1) % (tiles + 1)], turned[c])
            gx = jnp.where(inside, below - here[c], 0.0)
            gy = right - here[c]
            if c == tiles - 1:
                gy = jnp.where(last_col, 0.0, gy)
            if c == tiles:
                gy = jnp.where(outside, 0.0, gy)
            GX[at(s, c)] = gx
            GY[at(s, c)] = gy

    everywhere = tuple(range(tiles + 1))

    def over_strips(first, end, group, work):
        def body(i, carry):
            for j in range(group):
                work(first + i * group + j)
            return carry

        trips = (end - first) // group
        if trips:
            lax.fori_loop(0, trips, body, 0)
        for s in range(first + trips * group, end):
            work(s)

    def between(k):
        def advance(s):
            for c in everywhere:
                du, noisy = DU[at(s, c)], N[at(s, c)]
                new = (U[at(s, c)] if k else noisy) - du
                U[at(s, c)] = new
                UB[at(s, c)] = new - du
                H[at(s, c)] = F[at(s, c)] * (new - noisy)

        over_strips(0, strips, 2, advance)
        over_strips(0, strips, 4, lambda s: gradient_strip(UB, s, everywhere))

    own = slice(SUB, SUB + rows)
    edges, inner = [], []
    for i, (src, dst) in enumerate(((noisy_hbm, N), (fid_hbm, F))):
        for j, (part, group) in enumerate((
            (slice(0, LANE), edges), (slice(cols - LANE, cols), edges), (slice(LANE, cols - LANE), inner),
        )):
            group.append(pltpu.make_async_copy(src.at[:, part], dst.at[own, part], load_sem.at[i, j]))
    for load in edges + inner:
        load.start()

    CB[...] = jnp.zeros_like(CB)

    def chip_at(y, core, z, x):
        row = lax.rem(my_row // 2 + y + SIDE, SIDE) * 2 + lax.rem(my_row + core, 2)
        col = lax.rem(my_col // SIDE + z + SIDE, SIDE) * SIDE + lax.rem(my_col + x + SIDE, SIDE)
        return row, col

    near = (-1, 0, 1)
    around = [(y, c, z, x) for y in near for c in (0, 1) for z in near for x in near if y or c or z or x]
    around.sort(key=lambda at: -sum(abs(v) for v in at))
    barrier = pltpu.get_barrier_semaphore()
    for where in around:
        pl.semaphore_signal(barrier, inc=1, device_id=chip_at(*where), device_id_type=MESH)

    corners = [(y, 0, z, x) for y in (-1, 1) for z in (-1, 1) for x in (-1, 1)]

    def tell():
        for where in corners:
            pl.semaphore_signal(known, inc=1, device_id=chip_at(*where), device_id_type=MESH)

    def pack(b):
        at = pl.ds(SUB + b * LANE, LANE)
        lanes = lax.broadcasted_iota(jnp.int32, (LANE, LANE), 1)
        n0, n7 = N[at, 0:LANE], N[at, cols - LANE : cols]
        f0 = pltpu.roll(F[at, 0:LANE], 8, axis=1)
        f7 = pltpu.roll(F[at, cols - LANE : cols], LANE - 8, axis=1)
        low = jnp.where(lanes < 8, n0, f0)
        high = jnp.where(lanes >= LANE - 8, n7, f7)
        return jnp.where(lanes < LANE // 2, low, high).T

    low, high = slice(0, 16), slice(LANE - 16, LANE)
    mid = slice(LANE, LANE + rows)
    top, bottom = slice(0, LANE), slice(LANE + rows, 2 * LANE + rows)
    first, last = slice(0, LANE), slice(rows - LANE, rows)
    below_rows = slice(rows + SUB, rows + 2 * SUB)
    moves = []
    for src, dst in ((noisy_hbm, N), (fid_hbm, F)):
        moves.append((src.at[0:SUB, :], dst.at[below_rows, 0:cols], -1, 0))
        moves.append((src.at[rows - SUB : rows, :], dst.at[0:SUB, 0:cols], 1, 0))
    moves.append((QT.at[low, :], CB.at[low, mid], 0, -1))
    moves.append((QT.at[high, :], CB.at[high, mid], 0, 1))
    for side, step in ((low, -1), (high, 1)):
        moves.append((QT.at[side, last], CB.at[side, top], 1, step))
        moves.append((QT.at[side, first], CB.at[side, bottom], -1, step))
    halos = [
        pltpu.make_async_remote_copy(
            src_ref=src, dst_ref=dst, send_sem=halo_send.at[i], recv_sem=halo_recv.at[i],
            device_id=(row_at(a), col_at(b)), device_id_type=MESH,
        )
        for i, (src, dst, a, b) in enumerate(moves)
    ]
    pl.semaphore_wait(barrier, len(around))
    tell()
    for halo in halos[:4]:
        halo.start()
    for load in edges:
        load.wait()
    for b in range(rows // LANE):
        QT[:, b * LANE : (b + 1) * LANE] = pack(b)
    for halo in halos[4:]:
        halo.start()
    for load in inner:
        load.wait()

    over_strips(1, strips - 2, 4, lambda s: gradient_strip(N, s, everywhere[: tiles - 1]))

    for halo in halos:
        halo.wait_recv()

    def unpack(block, start, count, to):
        turned = block.T[start : start + count, :]
        lanes = lax.broadcasted_iota(jnp.int32, turned.shape, 1)
        edge = jnp.logical_or(lanes < 8, lanes >= LANE - 8)
        fid = jnp.where(
            lanes < LANE // 2, pltpu.roll(turned, LANE - 8, axis=1), pltpu.roll(turned, 8, axis=1)
        )
        N[to : to + count, cols : cols + LANE] = jnp.where(edge, turned, 0.0)
        F[to : to + count, cols : cols + LANE] = jnp.where(edge, fid, 1.0)

    unpack(CB[:, top], LANE - SUB, SUB, 0)
    for b in range(rows // LANE):
        unpack(CB[:, (b + 1) * LANE : (b + 2) * LANE], 0, LANE, SUB + b * LANE)
    unpack(CB[:, bottom], 0, SUB, SUB + rows)

    over_strips(1, strips - 2, 16, lambda s: gradient_strip(N, s, everywhere[tiles - 1 :]))
    for s in (0, strips - 2, strips - 1):
        gradient_strip(N, s, everywhere)

    def strip(k, s, carry, counted, tau, sigma, itau, isigma):
        prev_x, prev_w, acc_p, acc_d, acc_l = carry
        prev_x, prev_w = list(prev_x), list(prev_w)
        final = k == ITERS - 1
        first_strip = isinstance(s, int) and s == 1

        def dual_step(c):
            qx, qy = sigma * GX[at(s, c)], sigma * GY[at(s, c)]
            if k:
                px, py = PX[at(s, c)], PY[at(s, c)]
                qx, qy = px + qx, py + qy
            scale = lax.rsqrt(jnp.maximum(qx * qx + qy * qy, 1.0))
            nx, ny = qx * scale, qy * scale
            tx, ty = (px - nx, py - ny) if k else (-nx, -ny)
            return nx, ny, tx, ty, pltpu.roll(nx, 1, axis=0), pltpu.roll(ny, 1, axis=1)

        def primal_step(c, dual, left):
            nx, ny, tx, ty, rx, ry = dual
            div = (nx - jnp.where(sub_first, prev_x[c], rx)) + (ny - jnp.where(lane_first, left, ry))
            prev_x[c] = rx
            if k:
                du = (H[at(s, c)] - div) / (itau + F[at(s, c)])
            else:
                du = div / (-itau - F[at(s, c)])
            DU[at(s, c)] = du
            scaled = sigma * du
            wx, wy = tx + scaled, ty + scaled
            before = DV[at(s, c)] if k and counted and c < tiles else None
            if not final:
                PX[at(s, c)] = nx
                PY[at(s, c)] = ny
                if c < tiles:
                    DV[at(s, c)] = div
            elif counted and c < tiles:
                own = at(s - 1, c)
                dual_out[(0, *own)] = nx
                dual_out[(1, *own)] = ny
            rwx, rwy = pltpu.roll(wx, 1, axis=0), pltpu.roll(wy, 1, axis=1)
            upper = prev_w[c]
            prev_w[c] = rwx
            return div, du, scaled, before, upper, rwx, rwy

        def residual(got, left):
            div, du, scaled, before, upper, rwx, rwy = got
            primal = du * itau - div
            if before is not None:
                primal = primal + before
            return (
                jnp.abs(primal),
                jnp.abs(jnp.where(sub_first, upper, rwx) - scaled),
                jnp.abs(jnp.where(lane_first, left, rwy) - scaled),
            )

        before_last = dual_step(tiles - 1)
        halo = dual_step(tiles)
        halo_got = primal_step(tiles, halo, before_last[5])
        left, left_w = halo[5], halo_got[6]
        for c in range(tiles):
            dual = before_last if c == tiles - 1 else dual_step(c)
            got = primal_step(c, dual, left)
            if counted:
                primal, along, across = residual(got, left_w)
                if first_strip:
                    along = jnp.where(in_first_row, 0.0, along)
                acc_p = acc_p + primal
                if c == 0:
                    acc_l = acc_l + across
                    acc_d = acc_d + along
                else:
                    acc_d = acc_d + (along + across)
            left, left_w = dual[5], got[6]
        return tuple(prev_x), tuple(prev_w), acc_p, acc_d, acc_l

    offsets = [(a, b) for a in range(n_row) for b in range(n_col) if a or b]
    offsets.sort(key=lambda ab: -distance(ab))
    partners = [(row_at(a), col_at(b)) for a, b in offsets]
    me = my_row * n_col + my_col
    others = len(offsets)

    def reduce_start(k, primal, dual):
        half = LANE // 2
        both = jnp.where(lane < half, primal + pltpu.roll(primal, half, axis=1), dual + pltpu.roll(dual, half, axis=1))
        rb[k, me] = jnp.sum(both, axis=0, keepdims=True)
        for partner in partners:
            pltpu.make_async_remote_copy(
                src_ref=rb.at[k, me], dst_ref=rb.at[k, me],
                send_sem=red_send.at[k], recv_sem=red_recv.at[k],
                device_id=partner, device_id_type=MESH,
            ).start()

    def reduce_end(k):
        got = rb.at[k, 0:others]
        pltpu.make_async_copy(got, got, red_recv.at[k]).wait()
        parts = [rb[k, i] for i in range(others + 1)]
        while len(parts) > 1:
            parts = [a + b for a, b in zip(parts[::2], parts[1::2])]
        lower = lax.broadcasted_iota(jnp.int32, (1, LANE), 1) < LANE // 2
        primal = jnp.sum(jnp.where(lower, parts[0], 0.0), axis=1, keepdims=True)
        dual = jnp.sum(jnp.where(lower, 0.0, parts[0]), axis=1, keepdims=True)
        return primal, dual

    def finish(s):
        for c in range(tiles):
            u_out[at(s - 1, c)] = U[at(s, c)] - DU[at(s, c)]

    zero = jnp.zeros((SUB, LANE), f32)
    tau_one = jnp.full((1, 1), first_tau, f32)
    sigma_one = jnp.full((1, 1), step_product / first_tau, f32)
    for k in range(ITERS):
        def full(x):
            return jnp.broadcast_to(x, (SUB, LANE))

        steps = (full(tau_one), full(sigma_one), full(1.0 / tau_one), full(1.0 / sigma_one))
        none = (zero,) * (tiles + 1)
        carry = strip(k, 0, (none, none, zero, zero, zero), False, *steps)
        carry = strip(k, 1, carry, True, *steps)

        def body(i, carry, k=k, steps=steps):
            for j in range(UNROLL):
                carry = strip(k, 2 + i * UNROLL + j, carry, True, *steps)
            return carry

        whole = (strips - 3) // UNROLL
        carry = lax.fori_loop(0, whole, body, carry)
        for s in range(2 + whole * UNROLL, strips - 1):
            carry = strip(k, s, carry, True, *steps)
        _, _, primal, dual, at_first = carry
        dual = dual + jnp.where(jnp.logical_and(at_left, lane_first), 0.0, at_first)
        if k == 0:
            pl.semaphore_wait(known, len(corners))
        reduce_start(k, primal, dual * steps[3])
        if k < ITERS - 1:
            strip(k, strips - 1, carry, False, *steps)
            between(k)
        else:
            over_strips(1, strips - 1, 4, finish)
        primal, dual = reduce_end(k)
        ratio = jnp.log((primal / cells + epsilon) / (dual / cells + epsilon))
        rate = np.float32(adapt_rate * adapt_decay**k)
        tau_one = tau_one * jnp.exp(rate * ratio / (1.0 + jnp.abs(ratio)))
        sigma_one = step_product / tau_one
    tau_out[...] = jnp.broadcast_to(tau_one, tau_out.shape)

    for halo in halos:
        halo.wait_send()
    for k in range(ITERS):
        sent = rb.at[k, 0:others]
        pltpu.make_async_copy(sent, sent, red_send.at[k]).wait()


def write_kernel(u_ref, dual_ref, u_hbm, dual_hbm, sem):
    moves = [(u_ref, u_hbm), (dual_ref.at[0], dual_hbm.at[0]), (dual_ref.at[1], dual_hbm.at[1])]
    copies = [pltpu.make_async_copy(src, dst, sem.at[i]) for i, (src, dst) in enumerate(moves)]
    for copy in copies:
        copy.start()
    for copy in copies:
        copy.wait()


def written(current, dual):
    vmem, hbm = (pl.BlockSpec(memory_space=space) for space in (pltpu.VMEM, pltpu.HBM))
    return pl.pallas_call(
        write_kernel,
        out_shape=tuple(jax.ShapeDtypeStruct(x.shape, x.dtype) for x in (current, dual)),
        in_specs=[vmem, vmem],
        out_specs=(hbm, hbm),
        scratch_shapes=[pltpu.SemaphoreType.DMA((3,))],
        compiler_params=pltpu.CompilerParams(vmem_limit_bytes=8 * 1024 * 1024),
    )(current, dual)


def solution(mesh):
    n_row, n_col = mesh.shape["row"], mesh.shape["col"]

    def on_device(noisy, fidelity):
        rows, cols = noisy.shape
        f32 = jnp.float32
        padded = pltpu.VMEM((rows + 2 * SUB, cols + LANE), f32)
        cells = np.float32(rows * cols * n_row * n_col)
        vmem = pl.BlockSpec(memory_space=pltpu.VMEM)
        current, dual, tau = pl.pallas_call(
            functools.partial(kernel, n_row, n_col, cells),
            out_shape=(
                jax.ShapeDtypeStruct((rows, cols), f32),
                jax.ShapeDtypeStruct((2, rows, cols), f32),
                jax.ShapeDtypeStruct((1, LANE), f32),
            ),
            in_specs=[pl.BlockSpec(memory_space=pl.ANY)] * 2,
            out_specs=(vmem, vmem, vmem),
            scratch_shapes=[padded] * 11
            + [
                pltpu.VMEM((LANE, rows), f32),
                pltpu.VMEM((LANE, rows + 2 * LANE), f32),
                pltpu.VMEM((ITERS, n_row * n_col, 1, LANE), f32),
                pltpu.SemaphoreType.DMA((2, 3)),
                pltpu.SemaphoreType.DMA((10,)),
                pltpu.SemaphoreType.DMA((10,)),
                pltpu.SemaphoreType.DMA((ITERS,)),
                pltpu.SemaphoreType.DMA((ITERS,)),
                pltpu.SemaphoreType.REGULAR,
            ],
            compiler_params=pltpu.CompilerParams(
                collective_id=0, has_side_effects=True, vmem_limit_bytes=40 * 1024 * 1024
            ),
        )(*(pltpu.with_memory_space_constraint(x, pltpu.HBM) for x in (noisy, fidelity)))
        current, dual = written(current, dual)
        return current, dual, tau[0, 0]

    return jax.shard_map(
        on_device,
        mesh=mesh,
        in_specs=(P("row", "col"), P("row", "col")),
        out_specs=(P("row", "col"), P(None, "row", "col"), P()),
        check_vma=False,
    )
```

```python
import functools
import jax
import jax.numpy as jnp
import numpy as np
from jax import lax
from jax.experimental import pallas as pl
from jax.experimental.pallas import tpu as pltpu
from jax.sharding import PartitionSpec as P

ITERS = 4
SIDE = 4
MESH = pl.DeviceIdType.MESH

first_tau = np.float32(0.35)
step_product = np.float32(0.124)
adapt_rate = 0.5
adapt_decay = 0.9
epsilon = np.float32(1e-06)

SUB = 8
LANE = 128
UNROLL = 10


def kernel(
    n_row, n_col, per_cell,
    noisy_hbm, fid_hbm,
    u_out, dual_out, tau_out,
    N, F, U, H, UB, DU, PX, PY, GX, GY, DV, QT, CB, rb,
    load_sem, halo_send, halo_recv, red_send, red_recv, known,
):
    rows, cols = noisy_hbm.shape
    strips = rows // SUB + 2
    tiles = cols // LANE
    my_row, my_col = lax.axis_index("row"), lax.axis_index("col")
    f32 = jnp.float32

    def distance(ab):
        a, b = ab
        return sum(min(v % 4, 4 - v % 4) for v in (a // 2, b // 4, b % 4))

    def row_at(d):
        return lax.rem(my_row + d + n_row, n_row)

    def col_at(d):
        return lax.rem(my_col + d + n_col, n_col)

    sub = lax.broadcasted_iota(jnp.int32, (SUB, LANE), 0)
    lane = lax.broadcasted_iota(jnp.int32, (SUB, LANE), 1)
    sub_first, sub_last = sub == 0, sub == SUB - 1
    lane_first, lane_last = lane == 0, lane == LANE - 1

    def at(s, c):
        start = s * SUB if isinstance(s, int) else pl.multiple_of(s * SUB, SUB)
        return pl.ds(start, SUB), slice(c * LANE, (c + 1) * LANE)

    at_left, at_right = my_col == 0, my_col == n_col - 1
    last_col = jnp.logical_and(at_right, lane_last)
    outside = jnp.logical_and(at_left, lane >= LANE // 2)
    in_first_row = jnp.logical_and(my_row == 0, sub_first)

    def gradient_strip(field, s, which):
        cell = my_row * rows + (s - 1) * SUB + sub
        inside = jnp.logical_and(cell >= 0, cell < n_row * rows - 1)
        after = min(s + 1, strips - 1) if isinstance(s, int) else jnp.minimum(s + 1, strips - 1)
        here = {c: field[at(s, c)] for c in {c for w in which for c in (w, (w + 1) % (tiles + 1))}}
        turned = {c: pltpu.roll(h, LANE - 1, axis=1) for c, h in here.items()}
        for c in which:
            below = jnp.where(
                sub_last,
                pltpu.roll(field[at(after, c)], SUB - 1, axis=0),
                pltpu.roll(here[c], SUB - 1, axis=0),
            )
            right = jnp.where(lane_last, turned[(c + 1) % (tiles + 1)], turned[c])
            gx = jnp.where(inside, below - here[c], 0.0)
            gy = right - here[c]
            if c == tiles - 1:
                gy = jnp.where(last_col, 0.0, gy)
            if c == tiles:
                gy = jnp.where(outside, 0.0, gy)
            GX[at(s, c)] = gx
            GY[at(s, c)] = gy

    everywhere = tuple(range(tiles + 1))

    def over_strips(first, end, group, work):
        def body(i, carry):
            for j in range(group):
                work(first + i * group + j)
            return carry

        trips = (end - first) // group
        if trips:
            lax.fori_loop(0, trips, body, 0)
        for s in range(first + trips * group, end):
            work(s)

    def between(k):
        def advance(s):
            for c in everywhere:
                du, noisy = DU[at(s, c)], N[at(s, c)]
                new = (U[at(s, c)] if k else noisy) - du
                U[at(s, c)] = new
                UB[at(s, c)] = new - du
                H[at(s, c)] = F[at(s, c)] * (new - noisy)

        over_strips(0, strips, 2, advance)
        over_strips(0, strips, 4, lambda s: gradient_strip(UB, s, everywhere))

    own = slice(SUB, SUB + rows)
    edges, inner = [], []
    for i, (src, dst) in enumerate(((noisy_hbm, N), (fid_hbm, F))):
        for j, (part, group) in enumerate((
            (slice(0, LANE), edges), (slice(cols - LANE, cols), edges), (slice(LANE, cols - LANE), inner),
        )):
            group.append(pltpu.make_async_copy(src.at[:, part], dst.at[own, part], load_sem.at[i, j]))
    for load in edges + inner:
        load.start()

    CB[...] = jnp.zeros_like(CB)

    def chip_at(y, core, z, x):
        row = lax.rem(my_row // 2 + y + SIDE, SIDE) * 2 + lax.rem(my_row + core, 2)
        col = lax.rem(my_col // SIDE + z + SIDE, SIDE) * SIDE + lax.rem(my_col + x + SIDE, SIDE)
        return row, col

    near = (-1, 0, 1)
    around = [(y, c, z, x) for y in near for c in (0, 1) for z in near for x in near if y or c or z or x]
    around.sort(key=lambda at: -sum(abs(v) for v in at))
    barrier = pltpu.get_barrier_semaphore()
    for where in around:
        pl.semaphore_signal(barrier, inc=1, device_id=chip_at(*where), device_id_type=MESH)

    corners = [(y, 0, z, x) for y in (-1, 1) for z in (-1, 1) for x in (-1, 1)]

    def tell():
        for where in corners:
            pl.semaphore_signal(known, inc=1, device_id=chip_at(*where), device_id_type=MESH)

    def pack(b):
        at = pl.ds(SUB + b * LANE, LANE)
        lanes = lax.broadcasted_iota(jnp.int32, (LANE, LANE), 1)
        n0, n7 = N[at, 0:LANE], N[at, cols - LANE : cols]
        f0 = pltpu.roll(F[at, 0:LANE], 8, axis=1)
        f7 = pltpu.roll(F[at, cols - LANE : cols], LANE - 8, axis=1)
        low = jnp.where(lanes < 8, n0, f0)
        high = jnp.where(lanes >= LANE - 8, n7, f7)
        return jnp.where(lanes < LANE // 2, low, high).T

    low, high = slice(0, 16), slice(LANE - 16, LANE)
    mid = slice(LANE, LANE + rows)
    top, bottom = slice(0, LANE), slice(LANE + rows, 2 * LANE + rows)
    first, last = slice(0, LANE), slice(rows - LANE, rows)
    below_rows = slice(rows + SUB, rows + 2 * SUB)
    moves = []
    for src, dst in ((noisy_hbm, N), (fid_hbm, F)):
        moves.append((src.at[0:SUB, :], dst.at[below_rows, 0:cols], -1, 0))
        moves.append((src.at[rows - SUB : rows, :], dst.at[0:SUB, 0:cols], 1, 0))
    moves.append((QT.at[low, :], CB.at[low, mid], 0, -1))
    moves.append((QT.at[high, :], CB.at[high, mid], 0, 1))
    for side, step in ((low, -1), (high, 1)):
        moves.append((QT.at[side, last], CB.at[side, top], 1, step))
        moves.append((QT.at[side, first], CB.at[side, bottom], -1, step))
    halos = [
        pltpu.make_async_remote_copy(
            src_ref=src, dst_ref=dst, send_sem=halo_send.at[i], recv_sem=halo_recv.at[i],
            device_id=(row_at(a), col_at(b)), device_id_type=MESH,
        )
        for i, (src, dst, a, b) in enumerate(moves)
    ]
    pl.semaphore_wait(barrier, len(around))
    tell()
    for load in edges:
        load.wait()
    for b in range(rows // LANE):
        QT[:, b * LANE : (b + 1) * LANE] = pack(b)
    for halo in halos[6:] + halos[4:6] + halos[:4]:
        halo.start()
    for load in inner:
        load.wait()

    over_strips(1, strips - 2, 4, lambda s: gradient_strip(N, s, everywhere[: tiles - 1]))

    for halo in halos:
        halo.wait_recv()

    def unpack(block, start, count, to):
        turned = block.T[start : start + count, :]
        lanes = lax.broadcasted_iota(jnp.int32, turned.shape, 1)
        edge = jnp.logical_or(lanes < 8, lanes >= LANE - 8)
        fid = jnp.where(
            lanes < LANE // 2, pltpu.roll(turned, LANE - 8, axis=1), pltpu.roll(turned, 8, axis=1)
        )
        N[to : to + count, cols : cols + LANE] = jnp.where(edge, turned, 0.0)
        F[to : to + count, cols : cols + LANE] = jnp.where(edge, fid, 1.0)

    unpack(CB[:, top], LANE - SUB, SUB, 0)
    for b in range(rows // LANE):
        unpack(CB[:, (b + 1) * LANE : (b + 2) * LANE], 0, LANE, SUB + b * LANE)
    unpack(CB[:, bottom], 0, SUB, SUB + rows)

    over_strips(1, strips - 2, 16, lambda s: gradient_strip(N, s, everywhere[tiles - 1 :]))
    for s in (0, strips - 2, strips - 1):
        gradient_strip(N, s, everywhere)

    def strip(k, s, carry, counted, tau, sigma, itau, isigma):
        prev_x, prev_w, acc_p, acc_d, acc_l = carry
        prev_x, prev_w = list(prev_x), list(prev_w)
        final = k == ITERS - 1
        first_strip = isinstance(s, int) and s == 1

        def dual_step(c):
            qx, qy = sigma * GX[at(s, c)], sigma * GY[at(s, c)]
            if k:
                px, py = PX[at(s, c)], PY[at(s, c)]
                qx, qy = px + qx, py + qy
            scale = lax.rsqrt(jnp.maximum(qx * qx + qy * qy, 1.0))
            nx, ny = qx * scale, qy * scale
            tx, ty = (px - nx, py - ny) if k else (-nx, -ny)
            return nx, ny, tx, ty, pltpu.roll(nx, 1, axis=0), pltpu.roll(ny, 1, axis=1)

        def primal_step(c, dual, left):
            nx, ny, tx, ty, rx, ry = dual
            div = (nx - jnp.where(sub_first, prev_x[c], rx)) + (ny - jnp.where(lane_first, left, ry))
            prev_x[c] = rx
            if k:
                du = (H[at(s, c)] - div) / (itau + F[at(s, c)])
            else:
                du = div / (-itau - F[at(s, c)])
            DU[at(s, c)] = du
            scaled = sigma * du
            wx, wy = tx + scaled, ty + scaled
            before = DV[at(s, c)] if k and counted and c < tiles else None
            if not final:
                PX[at(s, c)] = nx
                PY[at(s, c)] = ny
                if c < tiles:
                    DV[at(s, c)] = div
            elif counted and c < tiles:
                own = at(s - 1, c)
                dual_out[(0, *own)] = nx
                dual_out[(1, *own)] = ny
            rwx, rwy = pltpu.roll(wx, 1, axis=0), pltpu.roll(wy, 1, axis=1)
            upper = prev_w[c]
            prev_w[c] = rwx
            return div, du, scaled, before, upper, rwx, rwy

        def residual(got, left):
            div, du, scaled, before, upper, rwx, rwy = got
            primal = du * itau - div
            if before is not None:
                primal = primal + before
            return (
                jnp.abs(primal),
                jnp.abs(jnp.where(sub_first, upper, rwx) - scaled),
                jnp.abs(jnp.where(lane_first, left, rwy) - scaled),
            )

        before_last = dual_step(tiles - 1)
        halo = dual_step(tiles)
        halo_got = primal_step(tiles, halo, before_last[5])
        left, left_w = halo[5], halo_got[6]
        for c in range(tiles):
            dual = before_last if c == tiles - 1 else dual_step(c)
            got = primal_step(c, dual, left)
            if counted:
                primal, along, across = residual(got, left_w)
                if first_strip:
                    along = jnp.where(in_first_row, 0.0, along)
                acc_p = acc_p + primal
                if c == 0:
                    acc_l = acc_l + across
                    acc_d = acc_d + along
                else:
                    acc_d = acc_d + (along + across)
            left, left_w = dual[5], got[6]
        return tuple(prev_x), tuple(prev_w), acc_p, acc_d, acc_l

    offsets = [(a, b) for a in range(n_row) for b in range(n_col) if a or b]
    offsets.sort(key=lambda ab: -distance(ab))
    partners = [(row_at(a), col_at(b)) for a, b in offsets]
    me = my_row * n_col + my_col
    others = len(offsets)

    def reduce_start(k, primal, dual):
        half = LANE // 2
        both = jnp.where(lane < half, primal + pltpu.roll(primal, half, axis=1), dual + pltpu.roll(dual, half, axis=1))
        rb[k, me] = jnp.sum(both, axis=0, keepdims=True)
        for partner in partners:
            pltpu.make_async_remote_copy(
                src_ref=rb.at[k, me], dst_ref=rb.at[k, me],
                send_sem=red_send.at[k], recv_sem=red_recv.at[k],
                device_id=partner, device_id_type=MESH,
            ).start()

    def reduce_end(k):
        got = rb.at[k, 0:others]
        pltpu.make_async_copy(got, got, red_recv.at[k]).wait()
        parts = [rb[k, i] for i in range(others + 1)]
        while len(parts) > 1:
            parts = [a + b for a, b in zip(parts[::2], parts[1::2])]
        lower = lax.broadcasted_iota(jnp.int32, (1, LANE), 1) < LANE // 2
        primal = jnp.sum(jnp.where(lower, parts[0], 0.0), axis=1, keepdims=True)
        dual = jnp.sum(jnp.where(lower, 0.0, parts[0]), axis=1, keepdims=True)
        return primal, dual

    def finish(s):
        for c in range(tiles):
            u_out[at(s - 1, c)] = U[at(s, c)] - DU[at(s, c)]

    zero = jnp.zeros((SUB, LANE), f32)
    tau_one = jnp.full((1, 1), first_tau, f32)
    sigma_one = jnp.full((1, 1), step_product / first_tau, f32)
    for k in range(ITERS):
        def full(x):
            return jnp.broadcast_to(x, (SUB, LANE))

        steps = (full(tau_one), full(sigma_one), full(1.0 / tau_one), full(1.0 / sigma_one))
        none = (zero,) * (tiles + 1)
        carry = strip(k, 0, (none, none, zero, zero, zero), False, *steps)
        carry = strip(k, 1, carry, True, *steps)

        def body(i, carry, k=k, steps=steps):
            for j in range(UNROLL):
                carry = strip(k, 2 + i * UNROLL + j, carry, True, *steps)
            return carry

        whole = (strips - 3) // UNROLL
        carry = lax.fori_loop(0, whole, body, carry)
        for s in range(2 + whole * UNROLL, strips - 1):
            carry = strip(k, s, carry, True, *steps)
        _, _, primal, dual, at_first = carry
        dual = dual + jnp.where(jnp.logical_and(at_left, lane_first), 0.0, at_first)
        if k == 0:
            pl.semaphore_wait(known, len(corners))
        reduce_start(k, primal, dual * steps[3])
        if k < ITERS - 1:
            strip(k, strips - 1, carry, False, *steps)
            between(k)
        else:
            over_strips(1, strips - 1, 4, finish)
        primal, dual = reduce_end(k)
        ratio = jnp.log((primal * per_cell + epsilon) / (dual * per_cell + epsilon))
        rate = np.float32(adapt_rate * adapt_decay**k)
        tau_one = tau_one * jnp.exp(rate * ratio / (1.0 + jnp.abs(ratio)))
        sigma_one = step_product / tau_one
    tau_out[...] = jnp.broadcast_to(tau_one, tau_out.shape)

    for halo in halos:
        halo.wait_send()
    for k in range(ITERS):
        sent = rb.at[k, 0:others]
        pltpu.make_async_copy(sent, sent, red_send.at[k]).wait()


def write_kernel(u_ref, dual_ref, u_hbm, dual_hbm, sem):
    moves = [(u_ref, u_hbm), (dual_ref.at[0], dual_hbm.at[0]), (dual_ref.at[1], dual_hbm.at[1])]
    copies = [pltpu.make_async_copy(src, dst, sem.at[i]) for i, (src, dst) in enumerate(moves)]
    for copy in copies:
        copy.start()
    for copy in copies:
        copy.wait()


def written(current, dual):
    vmem, hbm = (pl.BlockSpec(memory_space=space) for space in (pltpu.VMEM, pltpu.HBM))
    return pl.pallas_call(
        write_kernel,
        out_shape=tuple(jax.ShapeDtypeStruct(x.shape, x.dtype) for x in (current, dual)),
        in_specs=[vmem, vmem],
        out_specs=(hbm, hbm),
        scratch_shapes=[pltpu.SemaphoreType.DMA((3,))],
        compiler_params=pltpu.CompilerParams(vmem_limit_bytes=8 * 1024 * 1024),
    )(current, dual)


def solution(mesh):
    n_row, n_col = mesh.shape["row"], mesh.shape["col"]

    def on_device(noisy, fidelity):
        rows, cols = noisy.shape
        f32 = jnp.float32
        padded = pltpu.VMEM((rows + 2 * SUB, cols + LANE), f32)
        per_cell = np.float32(1.0 / (rows * cols * n_row * n_col))
        vmem = pl.BlockSpec(memory_space=pltpu.VMEM)
        current, dual, tau = pl.pallas_call(
            functools.partial(kernel, n_row, n_col, per_cell),
            out_shape=(
                jax.ShapeDtypeStruct((rows, cols), f32),
                jax.ShapeDtypeStruct((2, rows, cols), f32),
                jax.ShapeDtypeStruct((1, LANE), f32),
            ),
            in_specs=[pl.BlockSpec(memory_space=pl.ANY)] * 2,
            out_specs=(vmem, vmem, vmem),
            scratch_shapes=[padded] * 11
            + [
                pltpu.VMEM((LANE, rows), f32),
                pltpu.VMEM((LANE, rows + 2 * LANE), f32),
                pltpu.VMEM((ITERS, n_row * n_col, 1, LANE), f32),
                pltpu.SemaphoreType.DMA((2, 3)),
                pltpu.SemaphoreType.DMA((10,)),
                pltpu.SemaphoreType.DMA((10,)),
                pltpu.SemaphoreType.DMA((ITERS,)),
                pltpu.SemaphoreType.DMA((ITERS,)),
                pltpu.SemaphoreType.REGULAR,
            ],
            compiler_params=pltpu.CompilerParams(
                collective_id=0, has_side_effects=True, vmem_limit_bytes=40 * 1024 * 1024
            ),
        )(*(pltpu.with_memory_space_constraint(x, pltpu.HBM) for x in (noisy, fidelity)))
        current, dual = written(current, dual)
        return current, dual, tau[0, 0]

    return jax.shard_map(
        on_device,
        mesh=mesh,
        in_specs=(P("row", "col"), P("row", "col")),
        out_specs=(P("row", "col"), P(None, "row", "col"), P()),
        check_vma=False,
    )
```
